32 devices in a mesh: dom: 4 (over y, core), cls: 8 (over z, x).
Axes of the slice: x: 2, y: 2, z: 4, core: 2. Of those that a mesh axis runs over, the one named last changes fastest.
Arguments:
- particles: bfloat16 [1536, 64, 288], P(('dom', 'cls')), may hold values from -6 to 6
- references: bfloat16 [200, 64, 288], P('cls'), may hold values from -6 to 6
- class_block: int32 [1536, 1], P(('dom', 'cls')), may hold values from 0 to 7; in each aligned block of 48 rows (0 to 47, 48 to 95, ...) at most 12 rows name the same one
- class_local: int32 [1536], P(('dom', 'cls')), may hold values from 0 to 24
- rotation: int32 [1536], P(('dom', 'cls')), may hold values from 0 to 35
- shifts: int32 [1536, 2], P(('dom', 'cls')), may hold values from -5 to 5
- defocus: int32 [1536], P(('dom', 'cls')), may hold values from 0 to 15
Outputs:
- best_score: float32 [1536], P(('dom', 'cls'))
- class_average: float32 [200, 64, 288], P('cls', 'dom')
The draws below stay inside these ranges and needn't reach their ends.
Inputs may be any that keep to these rules, and one draw needn't show every extreme that they name: `class_block`: in the rows of one device no class block is named more than 12 times, and some class block is named exactly 12 times by some device.
All inputs are finite; a program needn't handle non-finite values.
Results may differ from the reference program's by a relative error of at most 0.0045.
Values may be sent and summed in bfloat16 or wider, within the bound.
A program may use at most 128 MiB of HBM per device.

```python
import math
import jax
import jax.numpy as jnp
import numpy as np
from jax import lax

CYCLES = 64
ANG = 144
ROT = 36
BOX = 128
NBINS = 16
SHIFT = 5
CLS_DEV = 25
P_DEV = 48
OWNERS = 8
CLASSES = 200
CAP = 12
PARTICLES = 1536


def touch_ends(drawn, rng, low, high):
    longest = drawn.shape.index(max(drawn.shape))
    spots = []
    for shift in (0, 1):
        where = [jax.random.randint(jax.random.fold_in(rng, axis), (), 0, length) for axis, length in enumerate(drawn.shape)]
        where[longest] = (where[longest] + shift) % drawn.shape[longest]
        spots.append(tuple(where))
    return drawn.at[spots[0]].set(low).at[spots[1]].set(high)


def steps_of(own_key, extent, cuts, low, top_value):
    gain, own = 1.0, jax.random.fold_in(own_key, 6)
    for dim, parts in cuts:
        heights = jnp.exp(jax.random.uniform(jax.random.fold_in(own, dim), (parts,), jnp.float32, low / len(cuts), top_value / len(cuts)))
        gain = gain * jnp.repeat(heights, extent[dim] // parts).reshape([-1 if axis == dim else 1 for axis in range(len(extent))])
    return gain


def shared_out(stream_key, own, number, rows, number_of, top, most, skew):
    order = jax.random.permutation(stream_key, number_of)
    crowded, usual = load_shares(number_of, rows * top, most, skew, True), load_shares(number_of, rows * top, most, skew, False)
    places = jnp.arange(number_of)

    def named(lengths, turn):
        used = int((lengths > 0).sum())
        fixed = max(1, used // 4)
        passed = fixed + (places - fixed + turn * (used - fixed)) % max(1, number_of - fixed)
        return jnp.zeros((number_of,), jnp.int32).at[order[jnp.where(places < fixed, places, passed)]].set(jnp.asarray(lengths, jnp.int32))

    lengths = jnp.where(number % 4 == 0, named(crowded, number // 4), named(usual, number - number // 4 - 1))
    mixed = jax.random.permutation(jax.random.fold_in(own, 3), number_of)
    donor, sink = mixed[0:number_of // 2 * 2:2], mixed[1:number_of // 2 * 2:2]
    margin = jnp.minimum(lengths[donor] - 1, most - lengths[sink]) // 2
    margin = jnp.where((donor == order[0]) | (sink == order[0]) | (lengths[sink] == 0), 0, jnp.maximum(margin, 0))
    passed = jax.random.randint(jax.random.fold_in(own, 4), (number_of // 2,), 0, 1 << 20) % (margin + 1)
    lengths = lengths.at[donor].add(-passed).at[sink].add(passed)
    members = jnp.searchsorted(jnp.cumsum(lengths), jnp.arange(rows * top), side="right").astype(jnp.int32)
    grid = members.reshape(top, rows).T
    grid = grid[jax.random.permutation(jax.random.fold_in(own, 1), rows)]
    turn = jax.random.randint(jax.random.fold_in(own, 2), (rows, 1), 0, top)
    return jnp.take_along_axis(grid, (jnp.arange(top)[None, :] + turn) % top, axis=1)


def load_shares(amount, total, most, skew, full):
    weights = [(1 << 20) // math.isqrt(rank ** skew) + 1 for rank in range(1, amount + 1)]
    largest = most if full else min(most, max(-(-total // amount), total * weights[0] // sum(weights)))
    least = 1 if total - largest >= amount - 1 else 0
    given, surplus = [largest] + [least] * (amount - 1), total - largest - least * (amount - 1)
    while surplus > 0:
        movable = [i for i in range(1, amount) if given[i] < largest] or [i for i in range(1, amount) if given[i] < most]
        pool, remaining = sum([weights[i] for i in movable]), surplus
        for i in movable:
            extra = min(most - given[i], max(1, remaining * weights[i] // pool), surplus)
            given[i] = given[i] + extra
            surplus = surplus - extra
    return np.array(given)


def normal_values(key, dims, scale, most, split=(), kind=jnp.bfloat16):
    entries = scale * jax.random.normal(key, dims, jnp.float32)
    if split:
        entries = entries * steps_of(key, dims, split, -0.22, 0.18)
    return jnp.clip(entries, -most, most).astype(kind)


def setup_inputs(seed: int = 0) -> dict:
    key_of = jax.random.split(jax.random.key(seed), 8)
    particles = normal_values(key_of[0], (PARTICLES, CYCLES, 2 * ANG), 1.0, 6.0, ((0, 32),))
    references = normal_values(key_of[1], (CLASSES, CYCLES, 2 * ANG), 1.0, 6.0, ((0, 8),))
    class_block_keys = jax.random.split(jax.random.fold_in(key_of[2], 1), PARTICLES // P_DEV)
    class_block_turns = jax.random.permutation(jax.random.fold_in(key_of[2], 3), PARTICLES // P_DEV)
    class_block = jax.vmap(lambda own, number: shared_out(jax.random.fold_in(key_of[2], 2), own, number, P_DEV, OWNERS, 1, CAP, 2))(class_block_keys, class_block_turns).reshape((PARTICLES, 1))
    class_local = touch_ends(jax.random.randint(key_of[3], (PARTICLES,), 0, CLS_DEV), jax.random.fold_in(key_of[3], 1), 0, CLS_DEV - 1).astype(jnp.int32)
    rotation = touch_ends(jax.random.randint(key_of[4], (PARTICLES,), 0, ROT), jax.random.fold_in(key_of[4], 1), 0, ROT - 1).astype(jnp.int32)
    shifts = touch_ends(jax.random.randint(key_of[5], (PARTICLES, 2), 0 - SHIFT, SHIFT + 1), jax.random.fold_in(key_of[5], 1), 0 - SHIFT, SHIFT).astype(jnp.int32)
    defocus = touch_ends(jax.random.randint(key_of[6], (PARTICLES,), 0, NBINS), jax.random.fold_in(key_of[6], 1), 0, NBINS - 1).astype(jnp.int32)
    return {"particles": particles, "references": references, "class_block": class_block, "class_local": class_local, "rotation": rotation, "shifts": shifts, "defocus": defocus}


EPSILON = 1e-06

def angle_table(angles):
    sample_index = jnp.arange(angles, dtype=jnp.int32)
    turn_count = sample_index[:, None] * sample_index[None, :] % angles
    angle_value = turn_count.astype(jnp.float32) * (2.0 * math.pi / angles)
    cosine = jnp.cos(angle_value)
    sine_part = jnp.sin(angle_value)
    upper_half = jnp.concatenate([cosine, -sine_part], axis=1)
    lower_half = jnp.concatenate([sine_part, cosine], axis=1)
    return jnp.concatenate([upper_half, lower_half], axis=0).astype(jnp.bfloat16)

def rotation_table(angles, rotations):
    rotate_step = angles // rotations
    harmonic = jnp.arange(angles, dtype=jnp.int32)
    rotate_index = jnp.arange(rotations, dtype=jnp.int32)
    turn_count = harmonic[:, None] * (rotate_step * rotate_index[None, :]) % angles
    angle_value = turn_count.astype(jnp.float32) * (2.0 * math.pi / angles)
    return jnp.stack([jnp.cos(angle_value), jnp.sin(angle_value)]) * (1.0 / angles)

def ctf_table(bins, cycle_count):
    radius = (jnp.arange(cycle_count, dtype=jnp.int32) + 1).astype(jnp.float32) / cycle_count
    defocus_level = jnp.arange(bins, dtype=jnp.int32).astype(jnp.float32) / bins
    phase = math.pi * (3.0 + 9.0 * defocus_level[:, None]) * (radius[None, :] * radius[None, :])
    return 0.995 * jnp.sin(phase) + 0.1 * jnp.cos(phase)

def ctf_rows(defocus, bins, cycle_count):
    defocus_hits = (defocus[:, None] == jnp.arange(bins, dtype=jnp.int32)[None, :]).astype(jnp.float32)
    return jnp.dot(defocus_hits, ctf_table(bins, cycle_count), precision=lax.Precision.HIGHEST)

def shift_phase(shifts, cycle_count, angles):
    angle_value = jnp.arange(angles, dtype=jnp.int32).astype(jnp.float32) * (2.0 * math.pi / angles)
    radius = jnp.arange(cycle_count, dtype=jnp.int32).astype(jnp.float32)
    shift_x = shifts[:, 0].astype(jnp.float32)
    shift_y = shifts[:, 1].astype(jnp.float32)
    along_beam = shift_x[:, None] * jnp.cos(angle_value)[None, :] + shift_y[:, None] * jnp.sin(angle_value)[None, :]
    return 2.0 * math.pi / BOX * radius[None, :, None] * along_beam[:, None, :]

def prepare(particles, rotation, shifts, defocus):
    particle_count, cycle_count, row_width = particles.shape
    angles = row_width // 2
    phase = shift_phase(shifts, cycle_count, angles)
    real_part = particles[:, :, :angles].astype(jnp.float32)
    imag_part = particles[:, :, angles:].astype(jnp.float32)
    cos_phase = jnp.cos(phase)
    sin_phase = jnp.sin(phase)
    shifted = jnp.concatenate([real_part * cos_phase - imag_part * sin_phase, real_part * sin_phase + imag_part * cos_phase], axis=2).astype(jnp.bfloat16)
    spectrum = jnp.dot(shifted.reshape(particle_count * cycle_count, row_width), angle_table(angles), preferred_element_type=jnp.float32).reshape(particle_count, cycle_count, row_width)
    contrast = ctf_rows(defocus, NBINS, cycle_count)
    weighted = (contrast[:, :, None] * spectrum).astype(jnp.bfloat16)
    rotate_step = angles // ROT
    harmonic = jnp.arange(angles, dtype=jnp.int32)
    turn_count = harmonic[None, :] * (rotate_step * rotation[:, None]) % angles
    angle_value = turn_count.astype(jnp.float32) * (2.0 * math.pi / angles)
    cos_rot = jnp.cos(angle_value)[:, None, :]
    sin_rot = jnp.sin(angle_value)[:, None, :]
    spec_real = spectrum[:, :, :angles]
    spec_imag = spectrum[:, :, angles:]
    turned = jnp.concatenate([spec_real * cos_rot - spec_imag * sin_rot, spec_real * sin_rot + spec_imag * cos_rot], axis=2)
    unrotated = (contrast[:, :, None] * turned).astype(jnp.bfloat16)
    return (contrast, weighted, unrotated)

def block_scores(weighted, contrast, harmonics, rotate_table):
    particle_count, cycle_count, row_width = weighted.shape
    angles = row_width // 2
    class_count = harmonics.shape[0]
    stacked = jnp.concatenate([weighted[:, :, :angles], weighted[:, :, angles:]], axis=1)
    harm_real = harmonics[:, :, :angles]
    harm_imag = harmonics[:, :, angles:]
    paired = jnp.concatenate([jnp.concatenate([harm_real, harm_imag], axis=1), jnp.concatenate([harm_imag, -harm_real], axis=1)], axis=0)
    folded = jnp.einsum('pjm,njm->pnm', stacked.astype(jnp.float32), paired.astype(jnp.float32), precision=lax.Precision.HIGHEST)
    correlation = jnp.einsum('pcnm,cmr->pnr', folded.reshape(particle_count, 2, class_count, angles), rotate_table, precision=lax.Precision.HIGHEST)
    real_wide = harm_real.astype(jnp.float32)
    imag_wide = harm_imag.astype(jnp.float32)
    energy = lax.optimization_barrier(jnp.sum(real_wide * real_wide + imag_wide * imag_wide, axis=2))
    ref_power = jnp.dot(contrast * contrast, energy.T, precision=lax.Precision.HIGHEST) / angles
    scores = correlation / jnp.sqrt(ref_power + EPSILON)[:, :, None]
    return lax.optimization_barrier(jnp.max(scores, axis=(1, 2)))

def reference(particles, references, class_block, class_local, rotation, shifts, defocus):
    particle_total, cycle_count, row_width = particles.shape
    angles = row_width // 2
    harmonics = jnp.dot(references.reshape(CLASSES * cycle_count, row_width), angle_table(angles), preferred_element_type=jnp.float32).reshape(CLASSES, cycle_count, row_width).astype(jnp.bfloat16)
    rotate_table = rotation_table(angles, ROT)
    class_ids = class_block[:, 0] * CLS_DEV + class_local
    blocks = particle_total // P_DEV

    def one_block(running, block_index):
        numerator, denominator = running
        first_row = block_index * P_DEV

        def take_rows(source):
            return lax.dynamic_slice_in_dim(source, first_row, P_DEV, 0)
        contrast, weighted, unrotated = prepare(take_rows(particles), take_rows(rotation), take_rows(shifts), take_rows(defocus))

        def per_class(best_score, class_index):
            harm_block = lax.dynamic_slice_in_dim(harmonics, class_index * CLS_DEV, CLS_DEV, 0)
            return (jnp.maximum(best_score, block_scores(weighted, contrast, harm_block, rotate_table)), None)
        best_score, ignored = lax.scan(per_class, jnp.full((P_DEV,), -1e+30, jnp.float32), jnp.arange(CLASSES // CLS_DEV, dtype=jnp.int32))
        block_ids = take_rows(class_ids)
        numerator = numerator + jax.ops.segment_sum(unrotated.astype(jnp.float32), block_ids, num_segments=CLASSES)
        denominator = denominator + jax.ops.segment_sum(contrast * contrast, block_ids, num_segments=CLASSES)
        return ((numerator, denominator), best_score)
    start_sums = (jnp.zeros((CLASSES, cycle_count, row_width), jnp.float32), jnp.zeros((CLASSES, cycle_count), jnp.float32))
    (numerator, denominator), best_score = lax.scan(one_block, start_sums, jnp.arange(blocks, dtype=jnp.int32))
    class_average = numerator / (denominator[:, :, None] + 1.0)
    return (best_score.reshape(particle_total), class_average)
```

```python
import functools
import math

import jax
import jax.numpy as jnp
from jax import lax
from jax.experimental import pallas as pl
from jax.experimental.pallas import tpu as pltpu
from jax.sharding import PartitionSpec as P

ROT = 36
BOX = 128
NBINS = 16


EPSILON = 1e-06


def angle_table(angles):
    sample_index = jnp.arange(angles, dtype=jnp.int32)
    turn_count = sample_index[:, None] * sample_index[None, :] % angles
    angle_value = turn_count.astype(jnp.float32) * (2.0 * math.pi / angles)
    cosine = jnp.cos(angle_value)
    sine_part = jnp.sin(angle_value)
    upper_half = jnp.concatenate([cosine, -sine_part], axis=1)
    lower_half = jnp.concatenate([sine_part, cosine], axis=1)
    return jnp.concatenate([upper_half, lower_half], axis=0).astype(jnp.bfloat16)


def ctf_table(bins, cycle_count):
    radius = (jnp.arange(cycle_count, dtype=jnp.int32) + 1).astype(jnp.float32) / cycle_count
    defocus_level = jnp.arange(bins, dtype=jnp.int32).astype(jnp.float32) / bins
    phase = math.pi * (3.0 + 9.0 * defocus_level[:, None]) * (radius[None, :] * radius[None, :])
    return 0.995 * jnp.sin(phase) + 0.1 * jnp.cos(phase)


def ctf_rows(defocus, bins, cycle_count):
    defocus_hits = (defocus[:, None] == jnp.arange(bins, dtype=jnp.int32)[None, :]).astype(
        jnp.float32
    )
    return jnp.dot(defocus_hits, ctf_table(bins, cycle_count), precision=lax.Precision.HIGHEST)


def phase_turns(shifts, cycle_count, angles):
    inner = 8
    outer = cycle_count // inner
    angle_value = jnp.arange(angles, dtype=jnp.int32).astype(jnp.float32) * (2.0 * math.pi / angles)
    along = (
        shifts[:, 0].astype(jnp.float32)[:, None] * jnp.cos(angle_value)[None, :]
        + shifts[:, 1].astype(jnp.float32)[:, None] * jnp.sin(angle_value)[None, :]
    ) * (2.0 * math.pi / BOX)
    fine = jnp.arange(inner, dtype=jnp.int32).astype(jnp.float32)[None, :, None] * along[:, None, :]
    coarse = (jnp.arange(outer, dtype=jnp.int32) * inner).astype(jnp.float32)[
        None, :, None
    ] * along[:, None, :]
    cf, sf = jnp.cos(fine)[:, None], jnp.sin(fine)[:, None]
    cc, sc = jnp.cos(coarse)[:, :, None], jnp.sin(coarse)[:, :, None]
    shape = (shifts.shape[0], cycle_count, angles)
    return (cf * cc - sf * sc).reshape(shape), (sf * cc + cf * sc).reshape(shape)


def prepare(particles, rotation, shifts, defocus):
    particle_count, cycle_count, row_width = particles.shape
    angles = row_width // 2
    cos_phase, sin_phase = phase_turns(shifts, cycle_count, angles)
    real_part = particles[:, :, :angles].astype(jnp.float32)
    imag_part = particles[:, :, angles:].astype(jnp.float32)
    shifted = jnp.concatenate(
        [
            real_part * cos_phase - imag_part * sin_phase,
            real_part * sin_phase + imag_part * cos_phase,
        ],
        axis=2,
    ).astype(jnp.bfloat16)
    spectrum = jnp.dot(
        shifted.reshape(particle_count * cycle_count, row_width),
        angle_table(angles),
        preferred_element_type=jnp.float32,
    ).reshape(particle_count, cycle_count, row_width)
    contrast = ctf_rows(defocus, NBINS, cycle_count)
    weighted = (contrast[:, :, None] * spectrum).astype(jnp.bfloat16)
    rotate_step = angles // ROT
    harmonic = jnp.arange(angles, dtype=jnp.int32)
    turn_count = harmonic[None, :] * (rotate_step * rotation[:, None]) % angles
    angle_value = turn_count.astype(jnp.float32) * (2.0 * math.pi / angles)
    cos_rot = jnp.cos(angle_value)[:, None, :]
    sin_rot = jnp.sin(angle_value)[:, None, :]
    spec_real = spectrum[:, :, :angles]
    spec_imag = spectrum[:, :, angles:]
    turned = jnp.concatenate(
        [spec_real * cos_rot - spec_imag * sin_rot, spec_real * sin_rot + spec_imag * cos_rot],
        axis=2,
    )
    unrotated = (contrast[:, :, None] * turned).astype(jnp.bfloat16)
    return (contrast, weighted, unrotated)


def rotation_major(rows, copies):
    count, cycles, width = rows.shape
    wide = rows.reshape(count, cycles, 2, copies, width // 2 // copies)
    return wide.transpose(4, 0, 2, 3, 1).reshape(width // 2 // copies, count, 2 * copies * cycles)


def remote(src, dst, send, recv, d, c):
    return pltpu.make_async_remote_copy(
        src_ref=src,
        dst_ref=dst,
        send_sem=send,
        recv_sem=recv,
        device_id=(d, c),
        device_id_type=pl.DeviceIdType.MESH,
    )


def spread_kernel(
    doms, owners, fine, h, e, u, lab, hg, eg, ug, lg,
    s1, r1, s2, r2, s3, r3, se, re, su, ru, sl, rl, own,
):
    d = lax.axis_index("dom")
    c = lax.axis_index("cls")
    quarter = h.shape[0] // 4
    inner = d % 4
    base = d - inner
    side = inner % 2
    row = inner // 2
    piece = (side * 2 + row) * quarter
    across = base + (1 - row) * 2 + side
    mate = base + row * 2 + (1 - side)
    plane = doms * fine
    slab = d * fine + c % fine
    first = c - c % fine
    barrier = pltpu.get_barrier_semaphore()
    for i in range(1, owners):
        pl.semaphore_signal(
            barrier, inc=1, device_id=(d, (c + i) % owners), device_id_type=pl.DeviceIdType.MESH
        )
    for i in range(1, plane):
        other = (slab + i) % plane
        pl.semaphore_signal(
            barrier,
            inc=1,
            device_id=(other // fine, first + other % fine),
            device_id_type=pl.DeviceIdType.MESH,
        )
    pl.semaphore_wait(barrier, owners - 1 + plane - 1)
    local = [
        pltpu.make_async_copy(h, hg.at[c], own.at[0]),
        pltpu.make_async_copy(e, eg.at[c], own.at[1]),
        pltpu.make_async_copy(u.at[slab], ug.at[slab], own.at[2]),
        pltpu.make_async_copy(lab, lg.at[slab], own.at[3]),
    ]
    ended = []
    for i in range(1, owners):
        to = (c + i) % owners
        copy = remote(
            h.at[pl.ds(piece, quarter)],
            hg.at[c, pl.ds(piece, quarter)],
            s1.at[i],
            r1.at[i],
            d,
            to,
        )
        copy.start()
        ended.append(copy)
    for i in range(1, owners):
        copy = remote(e, eg.at[c], se.at[i], re.at[i], d, (c + i) % owners)
        copy.start()
        ended.append((copy, remote(e, eg.at[(c + owners - i) % owners], se.at[i], re.at[i], d, c)))
    for i in range(1, plane):
        other = (slab + i) % plane
        source = (slab + plane - i) % plane
        to = (other // fine, first + other % fine)
        copy = remote(u.at[other], ug.at[slab], su.at[i], ru.at[i], *to)
        copy.start()
        ended.append((copy, remote(u.at[other], ug.at[source], su.at[i], ru.at[i], *to)))
        copy = remote(lab, lg.at[slab], sl.at[i], rl.at[i], *to)
        copy.start()
        ended.append((copy, remote(lab, lg.at[source], sl.at[i], rl.at[i], *to)))
    for copy in local:
        copy.start()
    half = 2 * quarter
    other_piece = (side * 2 + 1 - row) * quarter

    def to_mate(i):
        source = (c + owners - i) % owners
        arrived = hg.at[source, pl.ds(other_piece, quarter)]
        remote(arrived, arrived, s2.at[i], r2.at[i], across, c).wait_recv()
        part = hg.at[source, pl.ds(side * half, half)]
        copy = remote(part, part, s3.at[i], r3.at[i], mate, c)
        copy.start()
        taken = hg.at[source, pl.ds((1 - side) * half, half)]
        ended.append((copy, remote(taken, taken, s3.at[i], r3.at[i], mate, c)))

    for i in range(1, owners):
        source = (c + owners - i) % owners
        part = hg.at[source, pl.ds(piece, quarter)]
        remote(part, part, s1.at[i], r1.at[i], d, source).wait_recv()
        copy = remote(part, part, s2.at[i], r2.at[i], across, c)
        copy.start()
        ended.append(copy)
        if i > 1:
            to_mate(i - 1)
    to_mate(owners - 1)
    for copy in ended:
        if isinstance(copy, tuple):
            copy[0].wait_send()
            copy[1].wait_recv()
        else:
            copy.wait_send()
    for copy in local:
        copy.wait()


def spread(h, e, u, lab, doms, owners, fine):
    plane = doms * fine
    dma = pltpu.SemaphoreType.DMA
    anywhere = pl.BlockSpec(memory_space=pl.ANY)
    return pl.pallas_call(
        functools.partial(spread_kernel, doms, owners, fine),
        out_shape=(
            jax.ShapeDtypeStruct((owners,) + h.shape, h.dtype),
            jax.ShapeDtypeStruct((owners,) + e.shape, e.dtype),
            jax.ShapeDtypeStruct(u.shape, u.dtype),
            jax.ShapeDtypeStruct((plane,) + lab.shape, lab.dtype),
        ),
        in_specs=[anywhere] * 4,
        out_specs=(anywhere,) * 4,
        scratch_shapes=[dma((owners,))] * 8 + [dma((plane,))] * 4 + [dma((4,))],
        compiler_params=pltpu.CompilerParams(collective_id=0, has_side_effects=True),
    )(h, e, u, lab)


def owner_kernel(owners, sums, den, sums_out, den_out, s1, r1, s2, r2, own):
    d = lax.axis_index("dom")
    c = lax.axis_index("cls")
    barrier = pltpu.get_barrier_semaphore()
    for i in range(1, owners):
        pl.semaphore_signal(
            barrier, inc=1, device_id=(d, (c + i) % owners), device_id_type=pl.DeviceIdType.MESH
        )
    pl.semaphore_wait(barrier, owners - 1)
    local = [
        pltpu.make_async_copy(sums.at[c], sums_out.at[c], own.at[0]),
        pltpu.make_async_copy(den.at[c], den_out.at[c], own.at[1]),
    ]
    ended = []
    for i in range(1, owners):
        to = (c + i) % owners
        source = (c + owners - i) % owners
        for src, dst, send, recv in ((sums, sums_out, s1, r1), (den, den_out, s2, r2)):
            copy = remote(src.at[to], dst.at[c], send.at[i], recv.at[i], d, to)
            copy.start()
            ended.append(
                (copy, remote(src.at[to], dst.at[source], send.at[i], recv.at[i], d, to))
            )
    for copy in local:
        copy.start()
    for copy, arrival in ended:
        copy.wait_send()
        arrival.wait_recv()
    for copy in local:
        copy.wait()


def to_owners(sums, den, owners):
    dma = pltpu.SemaphoreType.DMA
    anywhere = pl.BlockSpec(memory_space=pl.ANY)
    return pl.pallas_call(
        functools.partial(owner_kernel, owners),
        out_shape=(
            jax.ShapeDtypeStruct(sums.shape, sums.dtype),
            jax.ShapeDtypeStruct(den.shape, den.dtype),
        ),
        in_specs=[anywhere] * 2,
        out_specs=(anywhere,) * 2,
        scratch_shapes=[dma((owners,))] * 4 + [dma((2,))],
        compiler_params=pltpu.CompilerParams(collective_id=1, has_side_effects=True),
    )(sums, den)


def largest_turn(take):
    columns = [[None] * 9 for _ in range(4)]
    for m2 in range(9):
        real, imag = [], []
        for m1 in range(4):
            x, y = take((9 * m1 + 4 * m2) % 36)
            real.append(x)
            imag.append(y)
        ar, ai = real[0] + real[2], imag[0] + imag[2]
        br, bi = real[0] - real[2], imag[0] - imag[2]
        cr, ci = real[1] + real[3], imag[1] + imag[3]
        dr, di = real[1] - real[3], imag[1] - imag[3]
        columns[0][m2] = (ar + cr, ai + ci)
        columns[1][m2] = (br + di, bi - dr)
        columns[2][m2] = (ar - cr, ai - ci)
        columns[3][m2] = (br - di, bi + dr)
    best = None
    for x in columns:
        even = [x[b][0] + x[9 - b][0] for b in range(1, 5)]
        odd = [x[b][1] - x[9 - b][1] for b in range(1, 5)]
        tops = [x[0][0] + even[0] + even[1] + even[2] + even[3]]
        for s in range(1, 5):
            total = x[0][0]
            turn = None
            for b in range(1, 5):
                step = 2.0 * math.pi * (b * s % 9) / 9
                total = total + even[b - 1] * math.cos(step)
                term = odd[b - 1] * math.sin(step)
                turn = term if turn is None else turn + term
            tops.append(total + jnp.abs(turn))
        for top in tops:
            best = top if best is None else jnp.maximum(best, top)
    return best


def score_kernel(lhs, hg, scale, out, folded, best):
    step = pl.program_id(0)
    owners, group, padded, depth = hg.shape
    rows = lhs.shape[1]
    count = rows // 2
    for g in range(group):
        block = hg[:, g].reshape(owners * padded, depth)
        folded[step * group + g] = lax.dot_general(
            lhs[g], block, (((1,), (1,)), ((), ())), preferred_element_type=jnp.float32
        )

    @pl.when(step == pl.num_programs(0) - 1)
    def _():
        def tile(t, carry):
            at = pl.ds(pl.multiple_of(t * 8, 8), 8)
            after = pl.ds(pl.multiple_of(count + t * 8, 8), 8)
            for lane in range(owners * padded // 128):
                cols = pl.ds(lane * 128, 128)

                def take(m):
                    return folded[m, at, cols], folded[m, after, cols]

                best[at, cols] = largest_turn(take)
            return carry

        lax.fori_loop(0, count // 8, tile, 0)
        power = scale[...]
        scores = jnp.where(power < 0.0, -1e30, best[...] * power)
        out[...] = jnp.broadcast_to(jnp.max(scores, axis=1, keepdims=True), out.shape)


def best_scores(lhs, hg, scale):
    turns, rows, depth = lhs.shape
    owners, _, padded, _ = hg.shape
    group = 4
    width = owners * padded
    return pl.pallas_call(
        score_kernel,
        grid=(turns // group,),
        out_shape=jax.ShapeDtypeStruct((rows // 2, 128), jnp.float32),
        in_specs=[
            pl.BlockSpec((group, rows, depth), lambda i: (i, 0, 0)),
            pl.BlockSpec((owners, group, padded, depth), lambda i: (0, i, 0, 0)),
            pl.BlockSpec((rows // 2, width), lambda i: (0, 0)),
        ],
        out_specs=pl.BlockSpec((rows // 2, 128), lambda i: (0, 0)),
        scratch_shapes=[
            pltpu.VMEM((turns, rows, width), jnp.float32),
            pltpu.VMEM((rows // 2, width), jnp.float32),
        ],
        compiler_params=pltpu.CompilerParams(vmem_limit_bytes=48 * 1024 * 1024),
    )(lhs, hg, scale)[:, 0]


def on_device(particles, references, class_block, class_local, rotation, shifts, defocus):
    particle_count, cycle_count, row_width = particles.shape
    angles = row_width // 2
    copies = angles // ROT
    dom_count = lax.axis_size("dom")
    owners = lax.axis_size("cls")
    per_owner = references.shape[0]
    padded = -(-per_owner // 16) * 16
    fine = 2 if owners % 2 == 0 else 1
    plane = dom_count * fine
    thin = cycle_count // plane
    contrast, weighted, unrotated = prepare(particles, rotation, shifts, defocus)
    turned = rotation_major(weighted, copies)
    half = turned.shape[2] // 2
    lhs = jnp.concatenate(
        [turned, jnp.concatenate([-turned[:, :, half:], turned[:, :, :half]], axis=2)], axis=1
    )
    harmonics = (
        jnp.dot(
            references.reshape(per_owner * cycle_count, row_width),
            angle_table(angles),
            preferred_element_type=jnp.float32,
        )
        .reshape(per_owner, cycle_count, row_width)
        .astype(jnp.bfloat16)
    )
    wide = harmonics.astype(jnp.float32)
    energy = jnp.sum(wide * wide, axis=2)
    energy = jnp.pad(energy, ((0, padded - per_owner), (0, -cycle_count % 128)))
    major = jnp.pad(rotation_major(harmonics, copies), ((0, 0), (0, padded - per_owner), (0, 0)))
    outbox = (
        unrotated.reshape(particle_count, plane, thin * row_width).transpose(1, 0, 2)
    )
    class_ids = class_block[:, 0] * per_owner + class_local
    labels = jnp.pad(jnp.stack([class_ids, defocus]), ((0, 6), (0, -particle_count % 128)))
    all_major, all_energy, inbox, inbox_labels = spread(
        major, energy, outbox, labels, dom_count, owners, fine
    )
    ids = inbox_labels[:, 0, :particle_count].reshape(-1)
    bins = inbox_labels[:, 1, :particle_count].reshape(-1)
    member = jnp.arange(owners * per_owner, dtype=jnp.int32)[:, None] == ids[None, :]
    sums = jnp.dot(
        member.astype(jnp.bfloat16),
        inbox.reshape(plane * particle_count, thin * row_width),
        preferred_element_type=jnp.float32,
    ).astype(jnp.bfloat16)
    slab = lax.axis_index("dom") * fine + lax.axis_index("cls") % fine
    table = ctf_table(NBINS, cycle_count)
    table = lax.dynamic_slice_in_dim(table * table, slab * thin, thin, 1)
    hits = (bins[:, None] == jnp.arange(NBINS, dtype=jnp.int32)[None, :]).astype(jnp.float32)
    squares = jnp.dot(hits, table, precision=lax.Precision.HIGHEST)
    den = jnp.dot(member.astype(jnp.float32), squares, precision=lax.Precision.HIGHEST)
    den = den.reshape(owners, per_owner, thin).transpose(0, 2, 1)
    den = jnp.pad(den, ((0, 0), (0, -thin % 8), (0, -per_owner % 128)))
    all_sums, all_den = to_owners(
        sums.reshape(owners, per_owner, thin * row_width), den, owners
    )
    numerator = jnp.sum(
        all_sums.astype(jnp.float32).reshape(owners // fine, fine, per_owner, thin, row_width),
        axis=0,
    )
    denominator = jnp.sum(
        all_den[:, :thin, :per_owner].reshape(owners // fine, fine, thin, per_owner), axis=0
    ).transpose(0, 2, 1)
    class_average = numerator / (denominator[:, :, :, None] + 1.0)
    class_average = class_average.transpose(1, 0, 2, 3).reshape(
        per_owner, fine * thin, row_width
    )
    power = (
        jnp.dot(
            contrast * contrast,
            all_energy[:, :, :cycle_count].reshape(owners * padded, cycle_count).T,
            precision=lax.Precision.HIGHEST,
        )
        / angles
    )
    used = jnp.arange(owners * padded, dtype=jnp.int32) % padded < per_owner
    scale = jnp.where(used[None, :], 1.0 / (angles * jnp.sqrt(power + EPSILON)), -1.0)
    return (best_scores(lhs, all_major, scale), class_average)


def solution(mesh):
    placed = (
        P(("dom", "cls"), None, None),
        P("cls", None, None),
        P(("dom", "cls"), None),
        P(("dom", "cls")),
        P(("dom", "cls")),
        P(("dom", "cls"), None),
        P(("dom", "cls")),
    )
    return jax.shard_map(
        on_device,
        mesh=mesh,
        in_specs=placed,
        out_specs=(P(("dom", "cls")), P("cls", "dom", None)),
        check_vma=False,
    )
```

```python
import functools
import math

import jax
import jax.numpy as jnp
from jax import lax
from jax.experimental import pallas as pl
from jax.experimental.pallas import tpu as pltpu
from jax.sharding import PartitionSpec as P

ROT = 36
BOX = 128
NBINS = 16


EPSILON = 1e-06


def angle_table(angles):
    sample_index = jnp.arange(angles, dtype=jnp.int32)
    turn_count = sample_index[:, None] * sample_index[None, :] % angles
    angle_value = turn_count.astype(jnp.float32) * (2.0 * math.pi / angles)
    cosine = jnp.cos(angle_value)
    sine_part = jnp.sin(angle_value)
    upper_half = jnp.concatenate([cosine, -sine_part], axis=1)
    lower_half = jnp.concatenate([sine_part, cosine], axis=1)
    return jnp.concatenate([upper_half, lower_half], axis=0).astype(jnp.bfloat16)


def ctf_table(bins, cycle_count):
    radius = (jnp.arange(cycle_count, dtype=jnp.int32) + 1).astype(jnp.float32) / cycle_count
    defocus_level = jnp.arange(bins, dtype=jnp.int32).astype(jnp.float32) / bins
    phase = math.pi * (3.0 + 9.0 * defocus_level[:, None]) * (radius[None, :] * radius[None, :])
    return 0.995 * jnp.sin(phase) + 0.1 * jnp.cos(phase)


def ctf_rows(defocus, bins, cycle_count):
    defocus_hits = (defocus[:, None] == jnp.arange(bins, dtype=jnp.int32)[None, :]).astype(
        jnp.float32
    )
    return jnp.dot(defocus_hits, ctf_table(bins, cycle_count), precision=lax.Precision.HIGHEST)


def phase_turns(shifts, cycle_count, angles):
    inner = 8
    outer = cycle_count // inner
    angle_value = jnp.arange(angles, dtype=jnp.int32).astype(jnp.float32) * (2.0 * math.pi / angles)
    along = (
        shifts[:, 0].astype(jnp.float32)[:, None] * jnp.cos(angle_value)[None, :]
        + shifts[:, 1].astype(jnp.float32)[:, None] * jnp.sin(angle_value)[None, :]
    ) * (2.0 * math.pi / BOX)
    fine = jnp.arange(inner, dtype=jnp.int32).astype(jnp.float32)[None, :, None] * along[:, None, :]
    coarse = (jnp.arange(outer, dtype=jnp.int32) * inner).astype(jnp.float32)[
        None, :, None
    ] * along[:, None, :]
    cf, sf = jnp.cos(fine)[:, None], jnp.sin(fine)[:, None]
    cc, sc = jnp.cos(coarse)[:, :, None], jnp.sin(coarse)[:, :, None]
    shape = (shifts.shape[0], cycle_count, angles)
    return (cf * cc - sf * sc).reshape(shape), (sf * cc + cf * sc).reshape(shape)


def prepare(particles, rotation, shifts, defocus):
    particle_count, cycle_count, row_width = particles.shape
    angles = row_width // 2
    cos_phase, sin_phase = phase_turns(shifts, cycle_count, angles)
    real_part = particles[:, :, :angles].astype(jnp.float32)
    imag_part = particles[:, :, angles:].astype(jnp.float32)
    shifted = jnp.concatenate(
        [
            real_part * cos_phase - imag_part * sin_phase,
            real_part * sin_phase + imag_part * cos_phase,
        ],
        axis=2,
    ).astype(jnp.bfloat16)
    spectrum = jnp.dot(
        shifted.reshape(particle_count * cycle_count, row_width),
        angle_table(angles),
        preferred_element_type=jnp.float32,
    ).reshape(particle_count, cycle_count, row_width)
    contrast = ctf_rows(defocus, NBINS, cycle_count)
    weighted = (contrast[:, :, None] * spectrum).astype(jnp.bfloat16)
    rotate_step = angles // ROT
    harmonic = jnp.arange(angles, dtype=jnp.int32)
    turn_count = harmonic[None, :] * (rotate_step * rotation[:, None]) % angles
    angle_value = turn_count.astype(jnp.float32) * (2.0 * math.pi / angles)
    cos_rot = jnp.cos(angle_value)[:, None, :]
    sin_rot = jnp.sin(angle_value)[:, None, :]
    spec_real = spectrum[:, :, :angles]
    spec_imag = spectrum[:, :, angles:]
    turned = jnp.concatenate(
        [spec_real * cos_rot - spec_imag * sin_rot, spec_real * sin_rot + spec_imag * cos_rot],
        axis=2,
    )
    unrotated = (contrast[:, :, None] * turned).astype(jnp.bfloat16)
    return (contrast, weighted, unrotated)


def rotation_major(rows, copies):
    count, cycles, width = rows.shape
    wide = rows.reshape(count, cycles, 2, copies, width // 2 // copies)
    return wide.transpose(4, 0, 2, 3, 1).reshape(width // 2 // copies, count, 2 * copies * cycles)


def remote(src, dst, send, recv, d, c):
    return pltpu.make_async_remote_copy(
        src_ref=src,
        dst_ref=dst,
        send_sem=send,
        recv_sem=recv,
        device_id=(d, c),
        device_id_type=pl.DeviceIdType.MESH,
    )


def place(h):
    d = lax.axis_index("dom")
    c = lax.axis_index("cls")
    inner = d % 4
    base = d - inner
    side = inner % 2
    row = inner // 2
    across = base + (1 - row) * 2 + side
    mate = base + row * 2 + (1 - side)
    return d, c, side, row, across, mate


def signal_to(barrier, d, c):
    pl.semaphore_signal(barrier, inc=1, device_id=(d, c), device_id_type=pl.DeviceIdType.MESH)


def finish(ended, local):
    for sent, arrival in ended:
        sent.wait_send()
        arrival.wait_recv()
    for copy in local:
        copy.wait()


def spread_kernel(
    doms, owners, fine, h, e, u, lab, hg, eg, ug, lg, s1, r1, se, re, su, ru, sl, rl, own
):
    d, c, side, row, across, mate = place(h)
    quarter = h.shape[0] // 4
    piece = (side * 2 + row) * quarter
    lines = owners // fine
    plane = doms * fine
    slab = d * fine + c % fine
    first = c - c % fine
    barrier = pltpu.get_barrier_semaphore()
    for i in range(1, owners):
        signal_to(barrier, d, (c + i) % owners)
    for i in range(1, plane):
        other = (slab + i) % plane
        signal_to(barrier, other // fine, first + other % fine)
    pl.semaphore_wait(barrier, owners - 1 + plane - 1)
    local = [
        pltpu.make_async_copy(h, hg.at[c], own.at[0]),
        pltpu.make_async_copy(e, eg.at[c], own.at[1]),
        pltpu.make_async_copy(u.at[slab], ug.at[slab], own.at[2]),
        pltpu.make_async_copy(lab, lg.at[slab], own.at[3]),
    ]
    ended = []

    def move(src, dst, at, source, send, recv, to):
        sent = remote(src, dst.at[at], send, recv, *to)
        sent.start()
        ended.append((sent, remote(src, dst.at[source], send, recv, *to)))

    part = pl.ds(piece, quarter)
    for i in range(1, plane):
        other = (slab + i) % plane
        source = (slab + plane - i) % plane
        to = (other // fine, first + other % fine)
        move(lab, lg, slab, source, sl.at[i], rl.at[i], to)
        move(u.at[other], ug, slab, source, su.at[i], ru.at[i], to)
    for i in range(1, lines):
        to = (c + i * fine) % owners
        source = (c + owners - i * fine) % owners
        sent = remote(h.at[part], hg.at[c, part], s1.at[i], r1.at[i], d, to)
        sent.start()
        ended.append((sent, remote(h.at[part], hg.at[source, part], s1.at[i], r1.at[i], d, to)))
    for i in range(1, owners):
        to = (c + i) % owners
        move(e, eg, c, (c + owners - i) % owners, se.at[i], re.at[i], (d, to))
    for copy in local:
        copy.start()
    finish(ended, local)


def spread(h, e, u, lab, doms, owners, fine):
    plane = doms * fine
    dma = pltpu.SemaphoreType.DMA
    anywhere = pl.BlockSpec(memory_space=pl.ANY)
    return pl.pallas_call(
        functools.partial(spread_kernel, doms, owners, fine),
        out_shape=(
            jax.ShapeDtypeStruct((owners,) + h.shape, h.dtype),
            jax.ShapeDtypeStruct((owners,) + e.shape, e.dtype),
            jax.ShapeDtypeStruct(u.shape, u.dtype),
            jax.ShapeDtypeStruct((plane,) + lab.shape, lab.dtype),
        ),
        in_specs=[anywhere] * 4,
        out_specs=(anywhere,) * 4,
        scratch_shapes=[dma((owners,))] * 4 + [dma((plane,))] * 4 + [dma((4,))],
        compiler_params=pltpu.CompilerParams(collective_id=0, has_side_effects=True),
    )(h, e, u, lab)


def owner_kernel(
    owners, fine, hg_in, sums, den, hg, sums_out, den_out,
    sx, rx, sy, ry, sm, rm, s1, r1, s2, r2, own,
):
    d, c, side, row, across, mate = place(hg)
    quarter = hg.shape[1] // 4
    half = 2 * quarter
    mine = pl.ds((side * 2 + row) * quarter, quarter)
    theirs = pl.ds((side * 2 + 1 - row) * quarter, quarter)
    here = pl.ds(side * half, half)
    there = pl.ds((1 - side) * half, half)
    lines = owners // fine
    barrier = pltpu.get_barrier_semaphore()
    for i in range(1, owners):
        signal_to(barrier, d, (c + i) % owners)
    signal_to(barrier, across, c)
    signal_to(barrier, mate, c)
    pl.semaphore_wait(barrier, owners + 1)
    local = [
        pltpu.make_async_copy(sums.at[c], sums_out.at[c], own.at[0]),
        pltpu.make_async_copy(den.at[c], den_out.at[c], own.at[1]),
    ]
    ended = []

    def shard(col, line):
        return (c - c % fine + line * fine + (c % fine + col) % fine) % owners

    def send(source, taken, part, other, sems, to):
        piece = hg.at[source, part]
        sent = remote(piece, piece, sems[0], sems[1], *to)
        sent.start()
        arrival = remote(piece, hg.at[taken, other], sems[0], sems[1], *to)
        ended.append((sent, arrival))
        return arrival

    def to_across(source, k):
        return send(source, source, mine, theirs, (sy.at[k], ry.at[k]), (across, c))

    def to_mate(source, k):
        send(source, source, here, there, (sm.at[k], rm.at[k]), (mate, c))

    from_side = []
    for col in range(1, fine):
        to = (d, c - c % fine + (c % fine + col) % fine)
        back = (fine - col) % fine
        for line in range(lines):
            k = col * lines + line
            from_side.append(
                (
                    shard(back, line),
                    k,
                    send(
                        shard(0, line),
                        shard(back, line),
                        mine,
                        mine,
                        (sx.at[k], rx.at[k]),
                        to,
                    ),
                )
            )
    waiting = []
    for line in range(1, lines):
        waiting.append((shard(0, line), line, to_across(shard(0, line), line)))
    for i in range(1, owners):
        to = (c + i) % owners
        source = (c + owners - i) % owners
        for src, dst, out, into in ((sums, sums_out, s1, r1), (den, den_out, s2, r2)):
            sent = remote(src.at[to], dst.at[c], out.at[i], into.at[i], d, to)
            sent.start()
            ended.append((sent, remote(src.at[to], dst.at[source], out.at[i], into.at[i], d, to)))
    for copy in local:
        copy.start()
    seen = set()
    for source, k, arrival in from_side:
        arrival.wait_recv()
        seen.add(id(arrival))
        waiting.append((source, k, to_across(source, k)))
        ready = waiting.pop(0)
        ready[2].wait_recv()
        seen.add(id(ready[2]))
        to_mate(ready[0], ready[1])
    for source, k, arrival in waiting:
        arrival.wait_recv()
        seen.add(id(arrival))
        to_mate(source, k)
    for sent, arrival in ended:
        sent.wait_send()
        if id(arrival) not in seen:
            arrival.wait_recv()
    for copy in local:
        copy.wait()


def to_owners(hg, sums, den, owners, fine):
    dma = pltpu.SemaphoreType.DMA
    anywhere = pl.BlockSpec(memory_space=pl.ANY)
    return pl.pallas_call(
        functools.partial(owner_kernel, owners, fine),
        out_shape=(
            jax.ShapeDtypeStruct(hg.shape, hg.dtype),
            jax.ShapeDtypeStruct(sums.shape, sums.dtype),
            jax.ShapeDtypeStruct(den.shape, den.dtype),
        ),
        in_specs=[anywhere] * 3,
        out_specs=(anywhere,) * 3,
        input_output_aliases={0: 0},
        scratch_shapes=[dma((owners,))] * 10 + [dma((2,))],
        compiler_params=pltpu.CompilerParams(collective_id=1, has_side_effects=True),
    )(hg, sums, den)


def largest_turn(take):
    columns = [[None] * 9 for _ in range(4)]
    for m2 in range(9):
        real, imag = [], []
        for m1 in range(4):
            x, y = take((9 * m1 + 4 * m2) % 36)
            real.append(x)
            imag.append(y)
        ar, ai = real[0] + real[2], imag[0] + imag[2]
        br, bi = real[0] - real[2], imag[0] - imag[2]
        cr, ci = real[1] + real[3], imag[1] + imag[3]
        dr, di = real[1] - real[3], imag[1] - imag[3]
        columns[0][m2] = (ar + cr, ai + ci)
        columns[1][m2] = (br + di, bi - dr)
        columns[2][m2] = (ar - cr, ai - ci)
        columns[3][m2] = (br - di, bi + dr)
    best = None
    for x in columns:
        even = [x[b][0] + x[9 - b][0] for b in range(1, 5)]
        odd = [x[b][1] - x[9 - b][1] for b in range(1, 5)]
        tops = [x[0][0] + even[0] + even[1] + even[2] + even[3]]
        for s in range(1, 5):
            total = x[0][0]
            turn = None
            for b in range(1, 5):
                step = 2.0 * math.pi * (b * s % 9) / 9
                total = total + even[b - 1] * math.cos(step)
                term = odd[b - 1] * math.sin(step)
                turn = term if turn is None else turn + term
            tops.append(total + jnp.abs(turn))
        for top in tops:
            best = top if best is None else jnp.maximum(best, top)
    return best


def score_kernel(lhs, hg, scale, out, folded, best):
    step = pl.program_id(0)
    owners, group, padded, depth = hg.shape
    rows = lhs.shape[1]
    count = rows // 2
    for g in range(group):
        block = hg[:, g].reshape(owners * padded, depth)
        folded[step * group + g] = lax.dot_general(
            lhs[g], block, (((1,), (1,)), ((), ())), preferred_element_type=jnp.float32
        )

    @pl.when(step == pl.num_programs(0) - 1)
    def _():
        def tile(t, carry):
            at = pl.ds(pl.multiple_of(t * 8, 8), 8)
            after = pl.ds(pl.multiple_of(count + t * 8, 8), 8)
            for lane in range(owners * padded // 128):
                cols = pl.ds(lane * 128, 128)

                def take(m):
                    return folded[m, at, cols], folded[m, after, cols]

                best[at, cols] = largest_turn(take)
            return carry

        lax.fori_loop(0, count // 8, tile, 0)
        power = scale[...]
        scores = jnp.where(power < 0.0, -1e30, best[...] * power)
        out[...] = jnp.broadcast_to(jnp.max(scores, axis=1, keepdims=True), out.shape)


def best_scores(lhs, hg, scale):
    turns, rows, depth = lhs.shape
    owners, _, padded, _ = hg.shape
    group = 4
    width = owners * padded
    return pl.pallas_call(
        score_kernel,
        grid=(turns // group,),
        out_shape=jax.ShapeDtypeStruct((rows // 2, 128), jnp.float32),
        in_specs=[
            pl.BlockSpec((group, rows, depth), lambda i: (i, 0, 0)),
            pl.BlockSpec((owners, group, padded, depth), lambda i: (0, i, 0, 0)),
            pl.BlockSpec((rows // 2, width), lambda i: (0, 0)),
        ],
        out_specs=pl.BlockSpec((rows // 2, 128), lambda i: (0, 0)),
        scratch_shapes=[
            pltpu.VMEM((turns, rows, width), jnp.float32),
            pltpu.VMEM((rows // 2, width), jnp.float32),
        ],
        compiler_params=pltpu.CompilerParams(vmem_limit_bytes=48 * 1024 * 1024),
    )(lhs, hg, scale)[:, 0]


def on_device(particles, references, class_block, class_local, rotation, shifts, defocus):
    particle_count, cycle_count, row_width = particles.shape
    angles = row_width // 2
    copies = angles // ROT
    dom_count = lax.axis_size("dom")
    owners = lax.axis_size("cls")
    per_owner = references.shape[0]
    padded = -(-per_owner // 16) * 16
    fine = 2 if owners % 2 == 0 else 1
    plane = dom_count * fine
    thin = cycle_count // plane
    contrast, weighted, unrotated = prepare(particles, rotation, shifts, defocus)
    turned = rotation_major(weighted, copies)
    half = turned.shape[2] // 2
    lhs = jnp.concatenate(
        [turned, jnp.concatenate([-turned[:, :, half:], turned[:, :, :half]], axis=2)], axis=1
    )
    harmonics = (
        jnp.dot(
            references.reshape(per_owner * cycle_count, row_width),
            angle_table(angles),
            preferred_element_type=jnp.float32,
        )
        .reshape(per_owner, cycle_count, row_width)
        .astype(jnp.bfloat16)
    )
    wide = harmonics.astype(jnp.float32)
    energy = jnp.sum(wide * wide, axis=2)
    energy = jnp.pad(energy, ((0, padded - per_owner), (0, -cycle_count % 128)))
    major = jnp.pad(rotation_major(harmonics, copies), ((0, 0), (0, padded - per_owner), (0, 0)))
    outbox = (
        unrotated.reshape(particle_count, plane, thin * row_width).transpose(1, 0, 2)
    )
    class_ids = class_block[:, 0] * per_owner + class_local
    labels = jnp.pad(jnp.stack([class_ids, defocus]), ((0, 6), (0, -particle_count % 128)))
    all_major, all_energy, inbox, inbox_labels = spread(
        major, energy, outbox, labels, dom_count, owners, fine
    )
    ids = inbox_labels[:, 0, :particle_count].reshape(-1)
    bins = inbox_labels[:, 1, :particle_count].reshape(-1)
    member = jnp.arange(owners * per_owner, dtype=jnp.int32)[:, None] == ids[None, :]
    sums = jnp.dot(
        member.astype(jnp.bfloat16),
        inbox.reshape(plane * particle_count, thin * row_width),
        preferred_element_type=jnp.float32,
    ).astype(jnp.bfloat16)
    slab = lax.axis_index("dom") * fine + lax.axis_index("cls") % fine
    table = ctf_table(NBINS, cycle_count)
    table = lax.dynamic_slice_in_dim(table * table, slab * thin, thin, 1)
    hits = (bins[:, None] == jnp.arange(NBINS, dtype=jnp.int32)[None, :]).astype(jnp.float32)
    squares = jnp.dot(hits, table, precision=lax.Precision.HIGHEST)
    den = jnp.dot(member.astype(jnp.float32), squares, precision=lax.Precision.HIGHEST)
    den = den.reshape(owners, per_owner, thin).transpose(0, 2, 1)
    den = jnp.pad(den, ((0, 0), (0, -thin % 8), (0, -per_owner % 128)))
    all_major, all_sums, all_den = to_owners(
        all_major, sums.reshape(owners, per_owner, thin * row_width), den, owners, fine
    )
    numerator = jnp.sum(
        all_sums.astype(jnp.float32).reshape(owners // fine, fine, per_owner, thin, row_width),
        axis=0,
    )
    denominator = jnp.sum(
        all_den[:, :thin, :per_owner].reshape(owners // fine, fine, thin, per_owner), axis=0
    ).transpose(0, 2, 1)
    class_average = numerator / (denominator[:, :, :, None] + 1.0)
    class_average = class_average.transpose(1, 0, 2, 3).reshape(
        per_owner, fine * thin, row_width
    )
    power = (
        jnp.dot(
            contrast * contrast,
            all_energy[:, :, :cycle_count].reshape(owners * padded, cycle_count).T,
            precision=lax.Precision.HIGHEST,
        )
        / angles
    )
    used = jnp.arange(owners * padded, dtype=jnp.int32) % padded < per_owner
    scale = jnp.where(used[None, :], 1.0 / (angles * jnp.sqrt(power + EPSILON)), -1.0)
    return (best_scores(lhs, all_major, scale), class_average)


def solution(mesh):
    placed = (
        P(("dom", "cls"), None, None),
        P("cls", None, None),
        P(("dom", "cls"), None),
        P(("dom", "cls")),
        P(("dom", "cls")),
        P(("dom", "cls"), None),
        P(("dom", "cls")),
    )
    return jax.shard_map(
        on_device,
        mesh=mesh,
        in_specs=placed,
        out_specs=(P(("dom", "cls")), P("cls", "dom", None)),
        check_vma=False,
    )
```

```python
import functools
import math

import jax
import jax.numpy as jnp
from jax import lax
from jax.experimental import pallas as pl
from jax.experimental.pallas import tpu as pltpu
from jax.sharding import PartitionSpec as P

ROT = 36
BOX = 128
NBINS = 16


EPSILON = 1e-06


def angle_table(angles):
    sample_index = jnp.arange(angles, dtype=jnp.int32)
    turn_count = sample_index[:, None] * sample_index[None, :] % angles
    angle_value = turn_count.astype(jnp.float32) * (2.0 * math.pi / angles)
    cosine = jnp.cos(angle_value)
    sine_part = jnp.sin(angle_value)
    upper_half = jnp.concatenate([cosine, -sine_part], axis=1)
    lower_half = jnp.concatenate([sine_part, cosine], axis=1)
    return jnp.concatenate([upper_half, lower_half], axis=0).astype(jnp.bfloat16)


def ctf_table(bins, cycle_count):
    radius = (jnp.arange(cycle_count, dtype=jnp.int32) + 1).astype(jnp.float32) / cycle_count
    defocus_level = jnp.arange(bins, dtype=jnp.int32).astype(jnp.float32) / bins
    phase = math.pi * (3.0 + 9.0 * defocus_level[:, None]) * (radius[None, :] * radius[None, :])
    return 0.995 * jnp.sin(phase) + 0.1 * jnp.cos(phase)


def ctf_rows(defocus, bins, cycle_count):
    defocus_hits = (defocus[:, None] == jnp.arange(bins, dtype=jnp.int32)[None, :]).astype(
        jnp.float32
    )
    return jnp.dot(defocus_hits, ctf_table(bins, cycle_count), precision=lax.Precision.HIGHEST)


def phase_turns(shifts, cycle_count, angles):
    inner = 8
    outer = cycle_count // inner
    angle_value = jnp.arange(angles, dtype=jnp.int32).astype(jnp.float32) * (2.0 * math.pi / angles)
    along = (
        shifts[:, 0].astype(jnp.float32)[:, None] * jnp.cos(angle_value)[None, :]
        + shifts[:, 1].astype(jnp.float32)[:, None] * jnp.sin(angle_value)[None, :]
    ) * (2.0 * math.pi / BOX)
    fine = jnp.arange(inner, dtype=jnp.int32).astype(jnp.float32)[None, :, None] * along[:, None, :]
    coarse = (jnp.arange(outer, dtype=jnp.int32) * inner).astype(jnp.float32)[
        None, :, None
    ] * along[:, None, :]
    cf, sf = jnp.cos(fine)[:, None], jnp.sin(fine)[:, None]
    cc, sc = jnp.cos(coarse)[:, :, None], jnp.sin(coarse)[:, :, None]
    shape = (shifts.shape[0], cycle_count, angles)
    return (cf * cc - sf * sc).reshape(shape), (sf * cc + cf * sc).reshape(shape)


def prepare(particles, rotation, shifts, defocus):
    particle_count, cycle_count, row_width = particles.shape
    angles = row_width // 2
    cos_phase, sin_phase = phase_turns(shifts, cycle_count, angles)
    real_part = particles[:, :, :angles].astype(jnp.float32)
    imag_part = particles[:, :, angles:].astype(jnp.float32)
    shifted = jnp.concatenate(
        [
            real_part * cos_phase - imag_part * sin_phase,
            real_part * sin_phase + imag_part * cos_phase,
        ],
        axis=2,
    ).astype(jnp.bfloat16)
    spectrum = jnp.dot(
        shifted.reshape(particle_count * cycle_count, row_width),
        angle_table(angles),
        preferred_element_type=jnp.float32,
    ).reshape(particle_count, cycle_count, row_width)
    contrast = ctf_rows(defocus, NBINS, cycle_count)
    rotate_step = angles // ROT
    harmonic = jnp.arange(angles, dtype=jnp.int32)
    turn_count = harmonic[None, :] * (rotate_step * rotation[:, None]) % angles
    angle_value = turn_count.astype(jnp.float32) * (2.0 * math.pi / angles)
    cos_rot = jnp.cos(angle_value)[:, None, :]
    sin_rot = jnp.sin(angle_value)[:, None, :]
    spec_real = spectrum[:, :, :angles]
    spec_imag = spectrum[:, :, angles:]
    turned = jnp.concatenate(
        [spec_real * cos_rot - spec_imag * sin_rot, spec_real * sin_rot + spec_imag * cos_rot],
        axis=2,
    )
    unrotated = (contrast[:, :, None] * turned).astype(jnp.bfloat16)
    return (contrast, shifted, unrotated)


def major_kernel(copies, both, rows, gain, table, out, energy, wide):
    pairs, lanes = gain.shape
    width = table.shape[0]
    turns = width // 2 // copies
    cycles = lanes // 2

    def transform(i, carry):
        both_rows = jnp.concatenate([rows[i], rows[pairs + i]], axis=0)
        spectrum = lax.dot_general(
            table[...],
            both_rows,
            (((1,), (1,)), ((), ())),
            preferred_element_type=jnp.float32,
        )
        spectrum = (spectrum * gain[pl.ds(i, 1), :]).astype(jnp.bfloat16).astype(jnp.float32)
        energy[pl.ds(i, 1), :] = jnp.sum(spectrum * spectrum, axis=0, keepdims=True)
        wide[pl.ds(i, width, stride=pairs), :] = spectrum
        return carry

    lax.fori_loop(0, pairs, transform, 0)
    low = lax.broadcasted_iota(jnp.int32, (pairs, lanes), 1) < cycles

    def gather(m, carry):
        def part(index):
            at = (index * turns + m) * pairs
            return wide[pl.ds(pl.multiple_of(at, 8), pairs), :]

        tops, ends = [], []
        for index in range(0, 2 * copies, 2):
            x, y = part(index), part(index + 1)
            tops.append(jnp.where(low, x, pltpu.roll(y, cycles, 1)))
            ends.append(jnp.where(low, pltpu.roll(x, cycles, 1), y))
        half = len(tops) // 2
        full = jnp.concatenate(
            [jnp.concatenate(tops, axis=1), jnp.concatenate(ends, axis=1)], axis=0
        )
        out[m, pl.ds(0, 2 * pairs), :] = full.astype(out.dtype)
        if both:
            tops = [-x for x in tops[half:]] + tops[:half]
            ends = [-x for x in ends[half:]] + ends[:half]
            full = jnp.concatenate(
                [jnp.concatenate(tops, axis=1), jnp.concatenate(ends, axis=1)], axis=0
            )
            out[m, pl.ds(2 * pairs, 2 * pairs), :] = full.astype(out.dtype)
        return carry

    lax.fori_loop(0, turns, gather, 0)


def rotation_major(rows, gain, table, copies, both):
    count, cycles, width = rows.shape
    pairs = count // 2
    turns = width // 2 // copies
    paired = jnp.concatenate([gain[:pairs], gain[pairs:]], axis=1)
    out, energy = pl.pallas_call(
        functools.partial(major_kernel, copies, both),
        out_shape=(
            jax.ShapeDtypeStruct((turns, count * (2 if both else 1), 2 * copies * cycles), rows.dtype),
            jax.ShapeDtypeStruct((pairs, 2 * cycles), jnp.float32),
        ),
        in_specs=[pl.BlockSpec(memory_space=pltpu.VMEM)] * 3,
        out_specs=(pl.BlockSpec(memory_space=pltpu.VMEM),) * 2,
        scratch_shapes=[pltpu.VMEM((width * pairs, 2 * cycles), jnp.float32)],
        compiler_params=pltpu.CompilerParams(vmem_limit_bytes=32 * 1024 * 1024),
    )(rows, paired, table)
    return out, jnp.concatenate([energy[:, :cycles], energy[:, cycles:]], axis=0)


def remote(src, dst, send, recv, d, c):
    return pltpu.make_async_remote_copy(
        src_ref=src,
        dst_ref=dst,
        send_sem=send,
        recv_sem=recv,
        device_id=(d, c),
        device_id_type=pl.DeviceIdType.MESH,
    )


def place(h):
    d = lax.axis_index("dom")
    c = lax.axis_index("cls")
    inner = d % 4
    base = d - inner
    side = inner % 2
    row = inner // 2
    across = base + (1 - row) * 2 + side
    mate = base + row * 2 + (1 - side)
    return d, c, side, row, across, mate


def signal_to(barrier, d, c):
    pl.semaphore_signal(barrier, inc=1, device_id=(d, c), device_id_type=pl.DeviceIdType.MESH)


def finish(ended, local):
    for sent, arrival in ended:
        sent.wait_send()
        arrival.wait_recv()
    for copy in local:
        copy.wait()


def spread_kernel(
    doms, owners, fine, h, e, u, lab, hg, eg, ug, lg, s1, r1, se, re, su, ru, sl, rl, own
):
    d, c, side, row, across, mate = place(h)
    quarter = h.shape[0] // 4
    piece = (side * 2 + row) * quarter
    lines = owners // fine
    plane = doms * fine
    slab = d * fine + c % fine
    first = c - c % fine
    barrier = pltpu.get_barrier_semaphore()
    for i in range(1, owners):
        signal_to(barrier, d, (c + i) % owners)
    for i in range(1, plane):
        other = (slab + i) % plane
        signal_to(barrier, other // fine, first + other % fine)
    pl.semaphore_wait(barrier, owners - 1 + plane - 1)
    local = [
        pltpu.make_async_copy(h, hg.at[c], own.at[0]),
        pltpu.make_async_copy(e, eg.at[c], own.at[1]),
        pltpu.make_async_copy(u.at[slab], ug.at[slab], own.at[2]),
        pltpu.make_async_copy(lab, lg.at[slab], own.at[3]),
    ]
    ended = []

    def move(src, dst, at, source, send, recv, to):
        sent = remote(src, dst.at[at], send, recv, *to)
        sent.start()
        ended.append((sent, remote(src, dst.at[source], send, recv, *to)))

    part = pl.ds(piece, quarter)
    for i in range(1, plane):
        other = (slab + i) % plane
        source = (slab + plane - i) % plane
        to = (other // fine, first + other % fine)
        move(lab, lg, slab, source, sl.at[i], rl.at[i], to)
        move(u.at[other], ug, slab, source, su.at[i], ru.at[i], to)
    for i in range(1, lines):
        to = (c + i * fine) % owners
        source = (c + owners - i * fine) % owners
        sent = remote(h.at[part], hg.at[c, part], s1.at[i], r1.at[i], d, to)
        sent.start()
        ended.append((sent, remote(h.at[part], hg.at[source, part], s1.at[i], r1.at[i], d, to)))
    for i in range(1, owners):
        to = (c + i) % owners
        move(e, eg, c, (c + owners - i) % owners, se.at[i], re.at[i], (d, to))
    for copy in local:
        copy.start()
    finish(ended, local)


def spread(h, e, u, lab, doms, owners, fine):
    plane = doms * fine
    dma = pltpu.SemaphoreType.DMA
    anywhere = pl.BlockSpec(memory_space=pl.ANY)
    return pl.pallas_call(
        functools.partial(spread_kernel, doms, owners, fine),
        out_shape=(
            jax.ShapeDtypeStruct((owners,) + h.shape, h.dtype),
            jax.ShapeDtypeStruct((owners,) + e.shape, e.dtype),
            jax.ShapeDtypeStruct(u.shape, u.dtype),
            jax.ShapeDtypeStruct((plane,) + lab.shape, lab.dtype),
        ),
        in_specs=[pl.BlockSpec(memory_space=pltpu.VMEM)] * 4,
        out_specs=(anywhere,) * 4,
        scratch_shapes=[dma((owners,))] * 4 + [dma((plane,))] * 4 + [dma((4,))],
        compiler_params=pltpu.CompilerParams(collective_id=0, has_side_effects=True),
    )(h, e, u, lab)


def owner_kernel(
    owners, fine, hg_in, sums, den, hg, sums_out, den_out,
    sx, rx, sy, ry, sm, rm, s1, r1, s2, r2, own,
):
    d, c, side, row, across, mate = place(hg)
    quarter = hg.shape[1] // 4
    half = 2 * quarter
    mine = pl.ds((side * 2 + row) * quarter, quarter)
    theirs = pl.ds((side * 2 + 1 - row) * quarter, quarter)
    here = pl.ds(side * half, half)
    there = pl.ds((1 - side) * half, half)
    lines = owners // fine
    barrier = pltpu.get_barrier_semaphore()
    for i in range(1, owners):
        signal_to(barrier, d, (c + i) % owners)
    signal_to(barrier, across, c)
    signal_to(barrier, mate, c)
    pl.semaphore_wait(barrier, owners + 1)
    local = [
        pltpu.make_async_copy(sums.at[c], sums_out.at[c], own.at[0]),
        pltpu.make_async_copy(den.at[c], den_out.at[c], own.at[1]),
    ]
    ended = []

    def shard(col, line):
        return (c - c % fine + line * fine + (c % fine + col) % fine) % owners

    def send(source, taken, part, other, sems, to):
        piece = hg.at[source, part]
        sent = remote(piece, piece, sems[0], sems[1], *to)
        sent.start()
        arrival = remote(piece, hg.at[taken, other], sems[0], sems[1], *to)
        ended.append((sent, arrival))
        return arrival

    def to_across(source, k):
        return send(source, source, mine, theirs, (sy.at[k], ry.at[k]), (across, c))

    def to_mate(source, k):
        send(source, source, here, there, (sm.at[k], rm.at[k]), (mate, c))

    from_side = []
    for col in range(1, fine):
        to = (d, c - c % fine + (c % fine + col) % fine)
        back = (fine - col) % fine
        for line in range(lines):
            k = col * lines + line
            from_side.append(
                (
                    shard(back, line),
                    k,
                    send(
                        shard(0, line),
                        shard(back, line),
                        mine,
                        mine,
                        (sx.at[k], rx.at[k]),
                        to,
                    ),
                )
            )
    waiting = []
    for line in range(1, lines):
        waiting.append((shard(0, line), line, to_across(shard(0, line), line)))
    for i in range(1, owners):
        to = (c + i) % owners
        source = (c + owners - i) % owners
        for src, dst, out, into in ((sums, sums_out, s1, r1), (den, den_out, s2, r2)):
            sent = remote(src.at[to], dst.at[c], out.at[i], into.at[i], d, to)
            sent.start()
            ended.append((sent, remote(src.at[to], dst.at[source], out.at[i], into.at[i], d, to)))
    for copy in local:
        copy.start()
    seen = set()
    for source, k, arrival in from_side:
        arrival.wait_recv()
        seen.add(id(arrival))
        waiting.append((source, k, to_across(source, k)))
        ready = waiting.pop(0)
        ready[2].wait_recv()
        seen.add(id(ready[2]))
        to_mate(ready[0], ready[1])
    for source, k, arrival in waiting:
        arrival.wait_recv()
        seen.add(id(arrival))
        to_mate(source, k)
    for sent, arrival in ended:
        sent.wait_send()
        if id(arrival) not in seen:
            arrival.wait_recv()
    for copy in local:
        copy.wait()


def to_owners(hg, sums, den, owners, fine):
    dma = pltpu.SemaphoreType.DMA
    anywhere = pl.BlockSpec(memory_space=pl.ANY)
    return pl.pallas_call(
        functools.partial(owner_kernel, owners, fine),
        out_shape=(
            jax.ShapeDtypeStruct(hg.shape, hg.dtype),
            jax.ShapeDtypeStruct(sums.shape, sums.dtype),
            jax.ShapeDtypeStruct(den.shape, den.dtype),
        ),
        in_specs=[anywhere] + [pl.BlockSpec(memory_space=pltpu.VMEM)] * 2,
        out_specs=(anywhere,) * 3,
        input_output_aliases={0: 0},
        scratch_shapes=[dma((owners,))] * 10 + [dma((2,))],
        compiler_params=pltpu.CompilerParams(collective_id=1, has_side_effects=True),
    )(hg, sums, den)


def largest_turn(take):
    columns = [[None] * 9 for _ in range(4)]
    for m2 in range(9):
        real, imag = [], []
        for m1 in range(4):
            x, y = take((9 * m1 + 4 * m2) % 36)
            real.append(x)
            imag.append(y)
        ar, ai = real[0] + real[2], imag[0] + imag[2]
        br, bi = real[0] - real[2], imag[0] - imag[2]
        cr, ci = real[1] + real[3], imag[1] + imag[3]
        dr, di = real[1] - real[3], imag[1] - imag[3]
        columns[0][m2] = (ar + cr, ai + ci)
        columns[1][m2] = (br + di, bi - dr)
        columns[2][m2] = (ar - cr, ai - ci)
        columns[3][m2] = (br - di, bi + dr)
    best = None
    for x in columns:
        even = [x[b][0] + x[9 - b][0] for b in range(1, 5)]
        odd = [x[b][1] - x[9 - b][1] for b in range(1, 5)]
        tops = [x[0][0] + even[0] + even[1] + even[2] + even[3]]
        for s in range(1, 5):
            total = x[0][0]
            turn = None
            for b in range(1, 5):
                step = 2.0 * math.pi * (b * s % 9) / 9
                total = total + even[b - 1] * math.cos(step)
                term = odd[b - 1] * math.sin(step)
                turn = term if turn is None else turn + term
            tops.append(total + jnp.abs(turn))
        for top in tops:
            best = top if best is None else jnp.maximum(best, top)
    return best


def score_kernel(lhs, hg, scale, out, folded, best):
    step = pl.program_id(0)
    owners, group, padded, depth = hg.shape
    rows = lhs.shape[1]
    count = rows // 2
    for g in range(group):
        block = hg[:, g].reshape(owners * padded, depth)
        folded[step * group + g] = lax.dot_general(
            lhs[g], block, (((1,), (1,)), ((), ())), preferred_element_type=jnp.float32
        )

    @pl.when(step == pl.num_programs(0) - 1)
    def _():
        def tile(t, carry):
            at = pl.ds(pl.multiple_of(t * 8, 8), 8)
            after = pl.ds(pl.multiple_of(count + t * 8, 8), 8)
            for lane in range(owners * padded // 128):
                cols = pl.ds(lane * 128, 128)

                def take(m):
                    return folded[m, at, cols], folded[m, after, cols]

                best[at, cols] = largest_turn(take)
            return carry

        lax.fori_loop(0, count // 8, tile, 0)
        power = scale[...]
        scores = jnp.where(power < 0.0, -1e30, best[...] * power)
        out[...] = jnp.broadcast_to(jnp.max(scores, axis=1, keepdims=True), out.shape)


def best_scores(lhs, hg, scale):
    turns, rows, depth = lhs.shape
    owners, _, padded, _ = hg.shape
    group = 4
    width = owners * padded
    return pl.pallas_call(
        score_kernel,
        grid=(turns // group,),
        out_shape=jax.ShapeDtypeStruct((rows // 2, 128), jnp.float32),
        in_specs=[
            pl.BlockSpec((group, rows, depth), lambda i: (i, 0, 0)),
            pl.BlockSpec((owners, group, padded, depth), lambda i: (0, i, 0, 0)),
            pl.BlockSpec((rows // 2, width), lambda i: (0, 0)),
        ],
        out_specs=pl.BlockSpec((rows // 2, 128), lambda i: (0, 0)),
        scratch_shapes=[
            pltpu.VMEM((turns, rows, width), jnp.float32),
            pltpu.VMEM((rows // 2, width), jnp.float32),
        ],
        compiler_params=pltpu.CompilerParams(vmem_limit_bytes=48 * 1024 * 1024),
    )(lhs, hg, scale)[:, 0]


def on_device(particles, references, class_block, class_local, rotation, shifts, defocus):
    particle_count, cycle_count, row_width = particles.shape
    angles = row_width // 2
    copies = angles // ROT
    dom_count = lax.axis_size("dom")
    owners = lax.axis_size("cls")
    per_owner = references.shape[0]
    padded = -(-per_owner // 16) * 16
    fine = 2 if owners % 2 == 0 else 1
    plane = dom_count * fine
    thin = cycle_count // plane
    contrast, shifted, unrotated = prepare(particles, rotation, shifts, defocus)
    table = angle_table(angles).T
    lhs, _ = rotation_major(shifted, contrast, table, copies, True)
    major, energy = rotation_major(
        jnp.pad(references, ((0, padded - per_owner), (0, 0), (0, 0))),
        jnp.ones((padded, cycle_count), jnp.float32),
        table,
        copies,
        False,
    )
    energy = jnp.pad(energy, ((0, 0), (0, -cycle_count % 128)))
    outbox = (
        unrotated.reshape(particle_count, plane, thin * row_width).transpose(1, 0, 2)
    )
    class_ids = class_block[:, 0] * per_owner + class_local
    labels = jnp.pad(jnp.stack([class_ids, defocus]), ((0, 6), (0, -particle_count % 128)))
    all_major, all_energy, inbox, inbox_labels = spread(
        major, energy, outbox, labels, dom_count, owners, fine
    )
    ids = inbox_labels[:, 0, :particle_count].reshape(-1)
    bins = inbox_labels[:, 1, :particle_count].reshape(-1)
    member = jnp.arange(owners * per_owner, dtype=jnp.int32)[:, None] == ids[None, :]
    sums = jnp.dot(
        member.astype(jnp.bfloat16),
        inbox.reshape(plane * particle_count, thin * row_width),
        preferred_element_type=jnp.float32,
    ).astype(jnp.bfloat16)
    slab = lax.axis_index("dom") * fine + lax.axis_index("cls") % fine
    table = ctf_table(NBINS, cycle_count)
    table = lax.dynamic_slice_in_dim(table * table, slab * thin, thin, 1)
    hits = (bins[:, None] == jnp.arange(NBINS, dtype=jnp.int32)[None, :]).astype(jnp.float32)
    squares = jnp.dot(hits, table, precision=lax.Precision.HIGHEST)
    den = jnp.dot(member.astype(jnp.float32), squares, precision=lax.Precision.HIGHEST)
    den = den.reshape(owners, per_owner, thin).transpose(0, 2, 1)
    den = jnp.pad(den, ((0, 0), (0, -thin % 8), (0, -per_owner % 128)))
    all_major, all_sums, all_den = to_owners(
        all_major, sums.reshape(owners, per_owner, thin * row_width), den, owners, fine
    )
    numerator = jnp.sum(
        all_sums.astype(jnp.float32).reshape(owners // fine, fine, per_owner, thin, row_width),
        axis=0,
    )
    denominator = jnp.sum(
        all_den[:, :thin, :per_owner].reshape(owners // fine, fine, thin, per_owner), axis=0
    ).transpose(0, 2, 1)
    class_average = numerator / (denominator[:, :, :, None] + 1.0)
    class_average = class_average.transpose(1, 0, 2, 3).reshape(
        per_owner, fine * thin, row_width
    )
    power = (
        jnp.dot(
            contrast * contrast,
            all_energy[:, :, :cycle_count].reshape(owners * padded, cycle_count).T,
            precision=lax.Precision.HIGHEST,
        )
        / angles
    )
    used = jnp.arange(owners * padded, dtype=jnp.int32) % padded < per_owner
    scale = jnp.where(used[None, :], 1.0 / (angles * jnp.sqrt(power + EPSILON)), -1.0)
    return (best_scores(lhs, all_major, scale), class_average)


def solution(mesh):
    placed = (
        P(("dom", "cls"), None, None),
        P("cls", None, None),
        P(("dom", "cls"), None),
        P(("dom", "cls")),
        P(("dom", "cls")),
        P(("dom", "cls"), None),
        P(("dom", "cls")),
    )
    return jax.shard_map(
        on_device,
        mesh=mesh,
        in_specs=placed,
        out_specs=(P(("dom", "cls")), P("cls", "dom", None)),
        check_vma=False,
    )
```

```python
import functools
import math

import jax
import jax.numpy as jnp
from jax import lax
from jax.experimental import pallas as pl
from jax.experimental.pallas import tpu as pltpu
from jax.sharding import PartitionSpec as P

ROT = 36
BOX = 128
NBINS = 16


EPSILON = 1e-06


def angle_table(angles):
    sample_index = jnp.arange(angles, dtype=jnp.int32)
    turn_count = sample_index[:, None] * sample_index[None, :] % angles
    angle_value = turn_count.astype(jnp.float32) * (2.0 * math.pi / angles)
    cosine = jnp.cos(angle_value)
    sine_part = jnp.sin(angle_value)
    upper_half = jnp.concatenate([cosine, -sine_part], axis=1)
    lower_half = jnp.concatenate([sine_part, cosine], axis=1)
    return jnp.concatenate([upper_half, lower_half], axis=0).astype(jnp.bfloat16)


def ctf_table(bins, cycle_count):
    radius = (jnp.arange(cycle_count, dtype=jnp.int32) + 1).astype(jnp.float32) / cycle_count
    defocus_level = jnp.arange(bins, dtype=jnp.int32).astype(jnp.float32) / bins
    phase = math.pi * (3.0 + 9.0 * defocus_level[:, None]) * (radius[None, :] * radius[None, :])
    return 0.995 * jnp.sin(phase) + 0.1 * jnp.cos(phase)


def ctf_rows(defocus, bins, cycle_count):
    defocus_hits = (defocus[:, None] == jnp.arange(bins, dtype=jnp.int32)[None, :]).astype(
        jnp.float32
    )
    return jnp.dot(defocus_hits, ctf_table(bins, cycle_count), precision=lax.Precision.HIGHEST)


def phase_turns(shifts, cycle_count, angles):
    inner = 8
    outer = cycle_count // inner
    angle_value = jnp.arange(angles, dtype=jnp.int32).astype(jnp.float32) * (2.0 * math.pi / angles)
    along = (
        shifts[:, 0].astype(jnp.float32)[:, None] * jnp.cos(angle_value)[None, :]
        + shifts[:, 1].astype(jnp.float32)[:, None] * jnp.sin(angle_value)[None, :]
    ) * (2.0 * math.pi / BOX)
    fine = jnp.arange(inner, dtype=jnp.int32).astype(jnp.float32)[None, :, None] * along[:, None, :]
    coarse = (jnp.arange(outer, dtype=jnp.int32) * inner).astype(jnp.float32)[
        None, :, None
    ] * along[:, None, :]
    cf, sf = jnp.cos(fine)[:, None], jnp.sin(fine)[:, None]
    cc, sc = jnp.cos(coarse)[:, :, None], jnp.sin(coarse)[:, :, None]
    shape = (shifts.shape[0], cycle_count, angles)
    return (cf * cc - sf * sc).reshape(shape), (sf * cc + cf * sc).reshape(shape)


def prepare(particles, rotation, shifts, defocus):
    particle_count, cycle_count, row_width = particles.shape
    angles = row_width // 2
    cos_phase, sin_phase = phase_turns(shifts, cycle_count, angles)
    real_part = particles[:, :, :angles].astype(jnp.float32)
    imag_part = particles[:, :, angles:].astype(jnp.float32)
    shifted = jnp.concatenate(
        [
            real_part * cos_phase - imag_part * sin_phase,
            real_part * sin_phase + imag_part * cos_phase,
        ],
        axis=2,
    ).astype(jnp.bfloat16)
    spectrum = jnp.dot(
        shifted.reshape(particle_count * cycle_count, row_width),
        angle_table(angles),
        preferred_element_type=jnp.float32,
    ).reshape(particle_count, cycle_count, row_width)
    contrast = ctf_rows(defocus, NBINS, cycle_count)
    rotate_step = angles // ROT
    harmonic = jnp.arange(angles, dtype=jnp.int32)
    turn_count = harmonic[None, :] * (rotate_step * rotation[:, None]) % angles
    angle_value = turn_count.astype(jnp.float32) * (2.0 * math.pi / angles)
    cos_rot = jnp.cos(angle_value)[:, None, :]
    sin_rot = jnp.sin(angle_value)[:, None, :]
    spec_real = spectrum[:, :, :angles]
    spec_imag = spectrum[:, :, angles:]
    turned = jnp.concatenate(
        [spec_real * cos_rot - spec_imag * sin_rot, spec_real * sin_rot + spec_imag * cos_rot],
        axis=2,
    )
    unrotated = (contrast[:, :, None] * turned).astype(jnp.bfloat16)
    return (contrast, shifted, unrotated)


def major_kernel(copies, packed, rows, gain, table, out, energy, wide, dense=None):
    pairs, lanes = gain.shape
    width = table.shape[0]
    turns = width // 2 // copies
    cycles = lanes // 2

    def transform(i, carry):
        both_rows = jnp.concatenate([rows[i], rows[pairs + i]], axis=0)
        spectrum = lax.dot_general(
            table[...],
            both_rows,
            (((1,), (1,)), ((), ())),
            preferred_element_type=jnp.float32,
        )
        spectrum = (spectrum * gain[pl.ds(i, 1), :]).astype(jnp.bfloat16).astype(jnp.float32)
        energy[pl.ds(i, 1), :] = jnp.sum(spectrum * spectrum, axis=0, keepdims=True)
        wide[pl.ds(i, width, stride=pairs), :] = spectrum
        return carry

    lax.fori_loop(0, pairs, transform, 0)
    low = lax.broadcasted_iota(jnp.int32, (pairs, lanes), 1) < cycles

    def gather(m, carry):
        def part(index):
            at = (index * turns + m) * pairs
            return wide[pl.ds(pl.multiple_of(at, 8), pairs), :]

        tops, ends = [], []
        for index in range(0, 2 * copies, 2):
            x, y = part(index), part(index + 1)
            tops.append(jnp.where(low, x, pltpu.roll(y, cycles, 1)))
            ends.append(jnp.where(low, pltpu.roll(x, cycles, 1), y))
        half = len(tops) // 2
        full = jnp.concatenate(
            [jnp.concatenate(tops, axis=1), jnp.concatenate(ends, axis=1)], axis=0
        )
        if packed:
            main = packed // 8 * 8
            group = turns // 4
            start = m // group * out.shape[1]
            turn = m % group
            at = pl.multiple_of(start + turn * main, 8)
            dense[pl.ds(at, main), :] = full[:main]
            for k in range(main, packed):
                at = start + group * main + turn * (packed - main) + k - main
                dense[pl.ds(at, 1), :] = full[k : k + 1]
        else:
            out[m, pl.ds(0, 2 * pairs), :] = full.astype(out.dtype)
            tops = [-x for x in tops[half:]] + tops[:half]
            ends = [-x for x in ends[half:]] + ends[:half]
            full = jnp.concatenate(
                [jnp.concatenate(tops, axis=1), jnp.concatenate(ends, axis=1)], axis=0
            )
            out[m, pl.ds(2 * pairs, 2 * pairs), :] = full.astype(out.dtype)
        return carry

    if packed:
        dense[...] = jnp.zeros_like(dense)
    lax.fori_loop(0, turns, gather, 0)
    if packed:
        out[...] = dense[...].reshape(out.shape).astype(out.dtype)


def rotation_major(rows, gain, table, copies, packed):
    count, cycles, width = rows.shape
    pairs = count // 2
    turns = width // 2 // copies
    paired = jnp.concatenate([gain[:pairs], gain[pairs:]], axis=1)
    depth = 2 * copies * cycles
    scratch = [pltpu.VMEM((width * pairs, 2 * cycles), jnp.float32)]
    shape = (turns, 2 * count, depth)
    if packed:
        shape = (4, -(-(turns // 4 * packed) // 8) * 8, depth)
        scratch.append(pltpu.VMEM((shape[0] * shape[1], depth), jnp.float32))
    out, energy = pl.pallas_call(
        functools.partial(major_kernel, copies, packed),
        out_shape=(
            jax.ShapeDtypeStruct(shape, rows.dtype),
            jax.ShapeDtypeStruct((pairs, 2 * cycles), jnp.float32),
        ),
        in_specs=[pl.BlockSpec(memory_space=pltpu.VMEM)] * 3,
        out_specs=(pl.BlockSpec(memory_space=pltpu.VMEM),) * 2,
        scratch_shapes=scratch,
        compiler_params=pltpu.CompilerParams(vmem_limit_bytes=32 * 1024 * 1024),
    )(rows, paired, table)
    return out, jnp.concatenate([energy[:, :cycles], energy[:, cycles:]], axis=0)


def remote(src, dst, send, recv, d, c):
    return pltpu.make_async_remote_copy(
        src_ref=src,
        dst_ref=dst,
        send_sem=send,
        recv_sem=recv,
        device_id=(d, c),
        device_id_type=pl.DeviceIdType.MESH,
    )


def place(h):
    d = lax.axis_index("dom")
    c = lax.axis_index("cls")
    inner = d % 4
    base = d - inner
    side = inner % 2
    row = inner // 2
    across = base + (1 - row) * 2 + side
    mate = base + row * 2 + (1 - side)
    return d, c, side, row, across, mate


def signal_to(barrier, d, c):
    pl.semaphore_signal(barrier, inc=1, device_id=(d, c), device_id_type=pl.DeviceIdType.MESH)


def finish(ended, local):
    for sent, arrival in ended:
        sent.wait_send()
        arrival.wait_recv()
    for copy in local:
        copy.wait()


def spread_kernel(
    doms, owners, fine, h, e, u, lab, hg, eg, ug, lg, s1, r1, se, re, su, ru, sl, rl, own
):
    d, c, side, row, across, mate = place(h)
    quarter = h.shape[0] // 4
    piece = (side * 2 + row) * quarter
    lines = owners // fine
    plane = doms * fine
    slab = d * fine + c % fine
    first = c - c % fine
    barrier = pltpu.get_barrier_semaphore()
    for i in range(1, owners):
        signal_to(barrier, d, (c + i) % owners)
    for i in range(1, plane):
        other = (slab + i) % plane
        signal_to(barrier, other // fine, first + other % fine)
    pl.semaphore_wait(barrier, owners - 1 + plane - 1)
    local = [
        pltpu.make_async_copy(h, hg.at[c], own.at[0]),
        pltpu.make_async_copy(e, eg.at[c], own.at[1]),
        pltpu.make_async_copy(u.at[slab], ug.at[slab], own.at[2]),
        pltpu.make_async_copy(lab, lg.at[slab], own.at[3]),
    ]
    ended = []

    def move(src, dst, at, source, send, recv, to):
        sent = remote(src, dst.at[at], send, recv, *to)
        sent.start()
        ended.append((sent, remote(src, dst.at[source], send, recv, *to)))

    part = pl.ds(piece, quarter)
    for i in range(1, plane):
        other = (slab + i) % plane
        source = (slab + plane - i) % plane
        to = (other // fine, first + other % fine)
        move(lab, lg, slab, source, sl.at[i], rl.at[i], to)
        move(u.at[other], ug, slab, source, su.at[i], ru.at[i], to)
    for i in range(1, lines):
        to = (c + i * fine) % owners
        source = (c + owners - i * fine) % owners
        sent = remote(h.at[part], hg.at[c, part], s1.at[i], r1.at[i], d, to)
        sent.start()
        ended.append((sent, remote(h.at[part], hg.at[source, part], s1.at[i], r1.at[i], d, to)))
    for i in range(1, owners):
        to = (c + i) % owners
        move(e, eg, c, (c + owners - i) % owners, se.at[i], re.at[i], (d, to))
    for copy in local:
        copy.start()
    finish(ended, local)


def spread(h, e, u, lab, doms, owners, fine):
    plane = doms * fine
    dma = pltpu.SemaphoreType.DMA
    anywhere = pl.BlockSpec(memory_space=pl.ANY)
    return pl.pallas_call(
        functools.partial(spread_kernel, doms, owners, fine),
        out_shape=(
            jax.ShapeDtypeStruct((owners,) + h.shape, h.dtype),
            jax.ShapeDtypeStruct((owners,) + e.shape, e.dtype),
            jax.ShapeDtypeStruct(u.shape, u.dtype),
            jax.ShapeDtypeStruct((plane,) + lab.shape, lab.dtype),
        ),
        in_specs=[pl.BlockSpec(memory_space=pltpu.VMEM)] * 4,
        out_specs=(anywhere,) * 4,
        scratch_shapes=[dma((owners,))] * 4 + [dma((plane,))] * 4 + [dma((4,))],
        compiler_params=pltpu.CompilerParams(collective_id=0, has_side_effects=True),
    )(h, e, u, lab)


def owner_kernel(
    owners, fine, hg_in, sums, den, hg, sums_out, den_out,
    sx, rx, sy, ry, sm, rm, s1, r1, s2, r2, own,
):
    d, c, side, row, across, mate = place(hg)
    quarter = hg.shape[1] // 4
    half = 2 * quarter
    mine = pl.ds((side * 2 + row) * quarter, quarter)
    theirs = pl.ds((side * 2 + 1 - row) * quarter, quarter)
    here = pl.ds(side * half, half)
    there = pl.ds((1 - side) * half, half)
    lines = owners // fine
    barrier = pltpu.get_barrier_semaphore()
    for i in range(1, owners):
        signal_to(barrier, d, (c + i) % owners)
    signal_to(barrier, across, c)
    signal_to(barrier, mate, c)
    pl.semaphore_wait(barrier, owners + 1)
    local = [
        pltpu.make_async_copy(sums.at[c], sums_out.at[c], own.at[0]),
        pltpu.make_async_copy(den.at[c], den_out.at[c], own.at[1]),
    ]
    ended = []

    def shard(col, line):
        return (c - c % fine + line * fine + (c % fine + col) % fine) % owners

    def send(source, taken, part, other, sems, to):
        piece = hg.at[source, part]
        sent = remote(piece, piece, sems[0], sems[1], *to)
        sent.start()
        arrival = remote(piece, hg.at[taken, other], sems[0], sems[1], *to)
        ended.append((sent, arrival))
        return arrival

    def to_across(source, k):
        return send(source, source, mine, theirs, (sy.at[k], ry.at[k]), (across, c))

    def to_mate(source, k):
        send(source, source, here, there, (sm.at[k], rm.at[k]), (mate, c))

    from_side = []
    for col in range(1, fine):
        to = (d, c - c % fine + (c % fine + col) % fine)
        back = (fine - col) % fine
        for line in range(lines):
            k = col * lines + line
            from_side.append(
                (
                    shard(back, line),
                    k,
                    send(
                        shard(0, line),
                        shard(back, line),
                        mine,
                        mine,
                        (sx.at[k], rx.at[k]),
                        to,
                    ),
                )
            )
    waiting = []
    for line in range(1, lines):
        waiting.append((shard(0, line), line, to_across(shard(0, line), line)))
    for i in range(1, owners):
        to = (c + i) % owners
        source = (c + owners - i) % owners
        for src, dst, out, into in ((sums, sums_out, s1, r1), (den, den_out, s2, r2)):
            sent = remote(src.at[to], dst.at[c], out.at[i], into.at[i], d, to)
            sent.start()
            ended.append((sent, remote(src.at[to], dst.at[source], out.at[i], into.at[i], d, to)))
    for copy in local:
        copy.start()
    seen = set()
    for source, k, arrival in from_side:
        arrival.wait_recv()
        seen.add(id(arrival))
        waiting.append((source, k, to_across(source, k)))
        ready = waiting.pop(0)
        ready[2].wait_recv()
        seen.add(id(ready[2]))
        to_mate(ready[0], ready[1])
    for source, k, arrival in waiting:
        arrival.wait_recv()
        seen.add(id(arrival))
        to_mate(source, k)
    for sent, arrival in ended:
        sent.wait_send()
        if id(arrival) not in seen:
            arrival.wait_recv()
    for copy in local:
        copy.wait()


def to_owners(hg, sums, den, owners, fine):
    dma = pltpu.SemaphoreType.DMA
    anywhere = pl.BlockSpec(memory_space=pl.ANY)
    return pl.pallas_call(
        functools.partial(owner_kernel, owners, fine),
        out_shape=(
            jax.ShapeDtypeStruct(hg.shape, hg.dtype),
            jax.ShapeDtypeStruct(sums.shape, sums.dtype),
            jax.ShapeDtypeStruct(den.shape, den.dtype),
        ),
        in_specs=[anywhere] + [pl.BlockSpec(memory_space=pltpu.VMEM)] * 2,
        out_specs=(anywhere,) * 3,
        input_output_aliases={0: 0},
        scratch_shapes=[dma((owners,))] * 10 + [dma((2,))],
        compiler_params=pltpu.CompilerParams(collective_id=1, has_side_effects=True),
    )(hg, sums, den)


def largest_turn(take):
    columns = [[None] * 9 for _ in range(4)]
    for m2 in range(9):
        real, imag = [], []
        for m1 in range(4):
            x, y = take((9 * m1 + 4 * m2) % 36)
            real.append(x)
            imag.append(y)
        ar, ai = real[0] + real[2], imag[0] + imag[2]
        br, bi = real[0] - real[2], imag[0] - imag[2]
        cr, ci = real[1] + real[3], imag[1] + imag[3]
        dr, di = real[1] - real[3], imag[1] - imag[3]
        columns[0][m2] = (ar + cr, ai + ci)
        columns[1][m2] = (br + di, bi - dr)
        columns[2][m2] = (ar - cr, ai - ci)
        columns[3][m2] = (br - di, bi + dr)
    best = None
    for x in columns:
        even = [x[b][0] + x[9 - b][0] for b in range(1, 5)]
        odd = [x[b][1] - x[9 - b][1] for b in range(1, 5)]
        tops = [x[0][0] + even[0] + even[1] + even[2] + even[3]]
        for s in range(1, 5):
            total = x[0][0]
            turn = None
            for b in range(1, 5):
                step = 2.0 * math.pi * (b * s % 9) / 9
                total = total + even[b - 1] * math.cos(step)
                term = odd[b - 1] * math.sin(step)
                turn = term if turn is None else turn + term
            tops.append(total + jnp.abs(turn))
        for top in tops:
            best = top if best is None else jnp.maximum(best, top)
    return best


def score_kernel(per_owner, lhs, hg, scale, out, folded, best):
    step = pl.program_id(0)
    owners, _, _, depth = hg.shape
    group, rows, _ = lhs.shape
    count = rows // 2
    width = folded.shape[2]
    main = per_owner // 8 * 8
    rest = per_owner - main
    tails = [hg[o, 0, group * main :, :].astype(jnp.float32) for o in range(owners)]
    for g in range(group):
        parts = [
            hg[o, 0, g * main : (g + 1) * main, :].astype(jnp.float32) for o in range(owners)
        ]
        parts += [tails[o][g * rest + k : g * rest + k + 1] for o in range(owners) for k in range(rest)]
        if width > owners * per_owner:
            parts.append(jnp.zeros((width - owners * per_owner, depth), jnp.float32))
        block = jnp.concatenate(parts, axis=0).astype(jnp.bfloat16)
        folded[step * group + g] = lax.dot_general(
            lhs[g], block, (((1,), (1,)), ((), ())), preferred_element_type=jnp.float32
        )

    @pl.when(step == pl.num_programs(0) - 1)
    def _():
        def tile(t, carry):
            at = pl.ds(pl.multiple_of(t * 8, 8), 8)
            after = pl.ds(pl.multiple_of(count + t * 8, 8), 8)
            for lane in range(width // 128):
                cols = pl.ds(lane * 128, 128)

                def take(m):
                    return folded[m, at, cols], folded[m, after, cols]

                best[at, cols] = largest_turn(take)
            return carry

        lax.fori_loop(0, count // 8, tile, 0)
        power = scale[...]
        scores = jnp.where(power < 0.0, -1e30, best[...] * power)
        out[...] = jnp.broadcast_to(jnp.max(scores, axis=1, keepdims=True), out.shape)


def best_scores(lhs, hg, scale, per_owner):
    turns, rows, depth = lhs.shape
    owners, pieces, packed, _ = hg.shape
    width = scale.shape[1]
    group = turns // pieces
    return pl.pallas_call(
        functools.partial(score_kernel, per_owner),
        grid=(pieces,),
        out_shape=jax.ShapeDtypeStruct((rows // 2, 128), jnp.float32),
        in_specs=[
            pl.BlockSpec((group, rows, depth), lambda i: (i, 0, 0)),
            pl.BlockSpec((owners, 1, packed, depth), lambda i: (0, i, 0, 0)),
            pl.BlockSpec((rows // 2, width), lambda i: (0, 0)),
        ],
        out_specs=pl.BlockSpec((rows // 2, 128), lambda i: (0, 0)),
        scratch_shapes=[
            pltpu.VMEM((turns, rows, width), jnp.float32),
            pltpu.VMEM((rows // 2, width), jnp.float32),
        ],
        compiler_params=pltpu.CompilerParams(vmem_limit_bytes=48 * 1024 * 1024),
    )(lhs, hg, scale)[:, 0]


def on_device(particles, references, class_block, class_local, rotation, shifts, defocus):
    particle_count, cycle_count, row_width = particles.shape
    angles = row_width // 2
    copies = angles // ROT
    dom_count = lax.axis_size("dom")
    owners = lax.axis_size("cls")
    per_owner = references.shape[0]
    padded = -(-per_owner // 16) * 16
    fine = 2 if owners % 2 == 0 else 1
    plane = dom_count * fine
    thin = cycle_count // plane
    contrast, shifted, unrotated = prepare(particles, rotation, shifts, defocus)
    table = angle_table(angles).T
    lhs, _ = rotation_major(shifted, contrast, table, copies, 0)
    major, energy = rotation_major(
        jnp.pad(references, ((0, padded - per_owner), (0, 0), (0, 0))),
        jnp.ones((padded, cycle_count), jnp.float32),
        table,
        copies,
        per_owner,
    )
    energy = jnp.pad(energy, ((0, 0), (0, -cycle_count % 128)))
    outbox = (
        unrotated.reshape(particle_count, plane, thin * row_width).transpose(1, 0, 2)
    )
    class_ids = class_block[:, 0] * per_owner + class_local
    labels = jnp.pad(jnp.stack([class_ids, defocus]), ((0, 6), (0, -particle_count % 128)))
    all_major, all_energy, inbox, inbox_labels = spread(
        major, energy, outbox, labels, dom_count, owners, fine
    )
    ids = inbox_labels[:, 0, :particle_count].reshape(-1)
    bins = inbox_labels[:, 1, :particle_count].reshape(-1)
    member = jnp.arange(owners * per_owner, dtype=jnp.int32)[:, None] == ids[None, :]
    sums = jnp.dot(
        member.astype(jnp.bfloat16),
        inbox.reshape(plane * particle_count, thin * row_width),
        preferred_element_type=jnp.float32,
    ).astype(jnp.bfloat16)
    slab = lax.axis_index("dom") * fine + lax.axis_index("cls") % fine
    table = ctf_table(NBINS, cycle_count)
    table = lax.dynamic_slice_in_dim(table * table, slab * thin, thin, 1)
    hits = (bins[:, None] == jnp.arange(NBINS, dtype=jnp.int32)[None, :]).astype(jnp.float32)
    squares = jnp.dot(hits, table, precision=lax.Precision.HIGHEST)
    den = jnp.dot(member.astype(jnp.float32), squares, precision=lax.Precision.HIGHEST)
    den = den.reshape(owners, per_owner, thin).transpose(0, 2, 1)
    den = jnp.pad(den, ((0, 0), (0, -thin % 8), (0, -per_owner % 128)))
    all_major, all_sums, all_den = to_owners(
        all_major, sums.reshape(owners, per_owner, thin * row_width), den, owners, fine
    )
    numerator = lax.optimization_barrier(
        jnp.sum(
            all_sums.astype(jnp.float32).reshape(
                owners // fine, fine, per_owner, thin * row_width
            ),
            axis=0,
        )
    ).reshape(fine, per_owner, thin, row_width)
    denominator = jnp.sum(
        all_den[:, :thin, :per_owner].reshape(owners // fine, fine, thin, per_owner), axis=0
    ).transpose(0, 2, 1)
    class_average = numerator / (denominator[:, :, :, None] + 1.0)
    class_average = class_average.transpose(1, 0, 2, 3).reshape(
        per_owner, fine * thin, row_width
    )
    main = per_owner // 8 * 8
    energies = jnp.concatenate(
        [
            all_energy[:, :main, :cycle_count].reshape(-1, cycle_count),
            all_energy[:, main:per_owner, :cycle_count].reshape(-1, cycle_count),
        ],
        axis=0,
    )
    power = jnp.dot(contrast * contrast, energies.T, precision=lax.Precision.HIGHEST) / angles
    scale = jnp.pad(
        1.0 / (angles * jnp.sqrt(power + EPSILON)),
        ((0, 0), (0, -owners * per_owner % 128)),
        constant_values=-1.0,
    )
    return (best_scores(lhs, all_major, scale, per_owner), class_average)


def solution(mesh):
    placed = (
        P(("dom", "cls"), None, None),
        P("cls", None, None),
        P(("dom", "cls"), None),
        P(("dom", "cls")),
        P(("dom", "cls")),
        P(("dom", "cls"), None),
        P(("dom", "cls")),
    )
    return jax.shard_map(
        on_device,
        mesh=mesh,
        in_specs=placed,
        out_specs=(P(("dom", "cls")), P("cls", "dom", None)),
        check_vma=False,
    )
```

```python
import functools
import math

import jax
import jax.numpy as jnp
from jax import lax
from jax.experimental import pallas as pl
from jax.experimental.pallas import tpu as pltpu
from jax.sharding import PartitionSpec as P

ROT = 36
BOX = 128
NBINS = 16


EPSILON = 1e-06


def angle_table(angles):
    sample_index = jnp.arange(angles, dtype=jnp.int32)
    turn_count = sample_index[:, None] * sample_index[None, :] % angles
    angle_value = turn_count.astype(jnp.float32) * (2.0 * math.pi / angles)
    cosine = jnp.cos(angle_value)
    sine_part = jnp.sin(angle_value)
    upper_half = jnp.concatenate([cosine, -sine_part], axis=1)
    lower_half = jnp.concatenate([sine_part, cosine], axis=1)
    return jnp.concatenate([upper_half, lower_half], axis=0).astype(jnp.bfloat16)


def ctf_table(bins, cycle_count):
    radius = (jnp.arange(cycle_count, dtype=jnp.int32) + 1).astype(jnp.float32) / cycle_count
    defocus_level = jnp.arange(bins, dtype=jnp.int32).astype(jnp.float32) / bins
    phase = math.pi * (3.0 + 9.0 * defocus_level[:, None]) * (radius[None, :] * radius[None, :])
    return 0.995 * jnp.sin(phase) + 0.1 * jnp.cos(phase)


def ctf_rows(defocus, bins, cycle_count):
    defocus_hits = (defocus[:, None] == jnp.arange(bins, dtype=jnp.int32)[None, :]).astype(
        jnp.float32
    )
    return jnp.dot(defocus_hits, ctf_table(bins, cycle_count), precision=lax.Precision.HIGHEST)


def phase_turns(shifts, cycle_count, angles):
    inner = 8
    outer = cycle_count // inner
    angle_value = jnp.arange(angles, dtype=jnp.int32).astype(jnp.float32) * (2.0 * math.pi / angles)
    along = (
        shifts[:, 0].astype(jnp.float32)[:, None] * jnp.cos(angle_value)[None, :]
        + shifts[:, 1].astype(jnp.float32)[:, None] * jnp.sin(angle_value)[None, :]
    ) * (2.0 * math.pi / BOX)
    fine = jnp.arange(inner, dtype=jnp.int32).astype(jnp.float32)[None, :, None] * along[:, None, :]
    coarse = (jnp.arange(outer, dtype=jnp.int32) * inner).astype(jnp.float32)[
        None, :, None
    ] * along[:, None, :]
    cf, sf = jnp.cos(fine)[:, None], jnp.sin(fine)[:, None]
    cc, sc = jnp.cos(coarse)[:, :, None], jnp.sin(coarse)[:, :, None]
    shape = (shifts.shape[0], cycle_count, angles)
    return (cf * cc - sf * sc).reshape(shape), (sf * cc + cf * sc).reshape(shape)


def prepare(particles, rotation, shifts, defocus):
    particle_count, cycle_count, row_width = particles.shape
    angles = row_width // 2
    cos_phase, sin_phase = phase_turns(shifts, cycle_count, angles)
    real_part = particles[:, :, :angles].astype(jnp.float32)
    imag_part = particles[:, :, angles:].astype(jnp.float32)
    shifted = jnp.concatenate(
        [
            real_part * cos_phase - imag_part * sin_phase,
            real_part * sin_phase + imag_part * cos_phase,
        ],
        axis=2,
    ).astype(jnp.bfloat16)
    spectrum = jnp.dot(
        shifted.reshape(particle_count * cycle_count, row_width),
        angle_table(angles),
        preferred_element_type=jnp.float32,
    ).reshape(particle_count, cycle_count, row_width)
    contrast = ctf_rows(defocus, NBINS, cycle_count)
    rotate_step = angles // ROT
    harmonic = jnp.arange(angles, dtype=jnp.int32)
    turn_count = harmonic[None, :] * (rotate_step * rotation[:, None]) % angles
    angle_value = turn_count.astype(jnp.float32) * (2.0 * math.pi / angles)
    cos_rot = jnp.cos(angle_value)[:, None, :]
    sin_rot = jnp.sin(angle_value)[:, None, :]
    spec_real = spectrum[:, :, :angles]
    spec_imag = spectrum[:, :, angles:]
    turned = jnp.concatenate(
        [spec_real * cos_rot - spec_imag * sin_rot, spec_real * sin_rot + spec_imag * cos_rot],
        axis=2,
    )
    unrotated = (contrast[:, :, None] * turned).astype(jnp.bfloat16)
    return (contrast, shifted, unrotated)


def major_kernel(copies, packed, rows, gain, table, out, energy, wide, dense=None):
    pairs, lanes = gain.shape
    width = table.shape[0]
    turns = width // 2 // copies
    cycles = lanes // 2

    def transform(i, carry):
        both_rows = jnp.concatenate([rows[i], rows[pairs + i]], axis=0)
        spectrum = lax.dot_general(
            table[...],
            both_rows,
            (((1,), (1,)), ((), ())),
            preferred_element_type=jnp.float32,
        )
        spectrum = (spectrum * gain[pl.ds(i, 1), :]).astype(jnp.bfloat16).astype(jnp.float32)
        energy[pl.ds(i, 1), :] = jnp.sum(spectrum * spectrum, axis=0, keepdims=True)
        wide[pl.ds(i, width, stride=pairs), :] = spectrum
        return carry

    lax.fori_loop(0, pairs, transform, 0, unroll=4)
    low = lax.broadcasted_iota(jnp.int32, (pairs, lanes), 1) < cycles

    def gather(m, carry):
        def part(index):
            at = (index * turns + m) * pairs
            return wide[pl.ds(pl.multiple_of(at, 8), pairs), :]

        tops, ends = [], []
        for index in range(0, 2 * copies, 2):
            x, y = part(index), part(index + 1)
            tops.append(jnp.where(low, x, pltpu.roll(y, cycles, 1)))
            ends.append(jnp.where(low, pltpu.roll(x, cycles, 1), y))
        half = len(tops) // 2
        full = jnp.concatenate(
            [jnp.concatenate(tops, axis=1), jnp.concatenate(ends, axis=1)], axis=0
        )
        if packed:
            main = packed // 8 * 8
            group = turns // 4
            start = m // group * out.shape[1]
            turn = m % group
            at = pl.multiple_of(start + turn * main, 8)
            dense[pl.ds(at, main), :] = full[:main]
            for k in range(main, packed):
                at = start + group * main + turn * (packed - main) + k - main
                dense[pl.ds(at, 1), :] = full[k : k + 1]
        else:
            out[m, pl.ds(0, 2 * pairs), :] = full.astype(out.dtype)
            tops = [-x for x in tops[half:]] + tops[:half]
            ends = [-x for x in ends[half:]] + ends[:half]
            full = jnp.concatenate(
                [jnp.concatenate(tops, axis=1), jnp.concatenate(ends, axis=1)], axis=0
            )
            out[m, pl.ds(2 * pairs, 2 * pairs), :] = full.astype(out.dtype)
        return carry

    if packed:
        dense[...] = jnp.zeros_like(dense)
    lax.fori_loop(0, turns, gather, 0, unroll=4)
    if packed:
        out[...] = dense[...].reshape(out.shape).astype(out.dtype)


def rotation_major(rows, gain, table, copies, packed):
    count, cycles, width = rows.shape
    pairs = count // 2
    turns = width // 2 // copies
    paired = jnp.concatenate([gain[:pairs], gain[pairs:]], axis=1)
    depth = 2 * copies * cycles
    scratch = [pltpu.VMEM((width * pairs, 2 * cycles), jnp.float32)]
    shape = (turns, 2 * count, depth)
    if packed:
        shape = (4, -(-(turns // 4 * packed) // 8) * 8, depth)
        scratch.append(pltpu.VMEM((shape[0] * shape[1], depth), jnp.float32))
    out, energy = pl.pallas_call(
        functools.partial(major_kernel, copies, packed),
        out_shape=(
            jax.ShapeDtypeStruct(shape, rows.dtype),
            jax.ShapeDtypeStruct((pairs, 2 * cycles), jnp.float32),
        ),
        in_specs=[pl.BlockSpec(memory_space=pltpu.VMEM)] * 3,
        out_specs=(pl.BlockSpec(memory_space=pltpu.VMEM),) * 2,
        scratch_shapes=scratch,
        compiler_params=pltpu.CompilerParams(vmem_limit_bytes=32 * 1024 * 1024),
    )(rows, paired, table)
    return out, jnp.concatenate([energy[:, :cycles], energy[:, cycles:]], axis=0)


def remote(src, dst, send, recv, d, c):
    return pltpu.make_async_remote_copy(
        src_ref=src,
        dst_ref=dst,
        send_sem=send,
        recv_sem=recv,
        device_id=(d, c),
        device_id_type=pl.DeviceIdType.MESH,
    )


def place(h):
    d = lax.axis_index("dom")
    c = lax.axis_index("cls")
    inner = d % 4
    base = d - inner
    side = inner % 2
    row = inner // 2
    across = base + (1 - row) * 2 + side
    mate = base + row * 2 + (1 - side)
    return d, c, side, row, across, mate


def signal_to(barrier, d, c):
    pl.semaphore_signal(barrier, inc=1, device_id=(d, c), device_id_type=pl.DeviceIdType.MESH)


def finish(ended, local):
    for sent, arrival in ended:
        sent.wait_send()
        arrival.wait_recv()
    for copy in local:
        copy.wait()


def spread_kernel(
    doms, owners, fine, h, e, u, lab, hg, eg, ug, lg, s1, r1, se, re, su, ru, sl, rl, own
):
    d, c, side, row, across, mate = place(h)
    quarter = h.shape[0] // 4
    piece = (side * 2 + row) * quarter
    lines = owners // fine
    plane = doms * fine
    slab = d * fine + c % fine
    first = c - c % fine
    barrier = pltpu.get_barrier_semaphore()
    for i in range(1, owners):
        signal_to(barrier, d, (c + i) % owners)
    for i in range(1, plane):
        other = (slab + i) % plane
        signal_to(barrier, other // fine, first + other % fine)
    pl.semaphore_wait(barrier, owners - 1 + plane - 1)
    local = [
        pltpu.make_async_copy(h, hg.at[c], own.at[0]),
        pltpu.make_async_copy(e, eg.at[c], own.at[1]),
        pltpu.make_async_copy(u.at[slab], ug.at[slab], own.at[2]),
        pltpu.make_async_copy(lab, lg.at[slab], own.at[3]),
    ]
    ended = []

    def move(src, dst, at, source, send, recv, to):
        sent = remote(src, dst.at[at], send, recv, *to)
        sent.start()
        ended.append((sent, remote(src, dst.at[source], send, recv, *to)))

    part = pl.ds(piece, quarter)
    for i in range(1, plane):
        other = (slab + i) % plane
        source = (slab + plane - i) % plane
        to = (other // fine, first + other % fine)
        move(lab, lg, slab, source, sl.at[i], rl.at[i], to)
        move(u.at[other], ug, slab, source, su.at[i], ru.at[i], to)
    for i in range(1, lines):
        to = (c + i * fine) % owners
        source = (c + owners - i * fine) % owners
        sent = remote(h.at[part], hg.at[c, part], s1.at[i], r1.at[i], d, to)
        sent.start()
        ended.append((sent, remote(h.at[part], hg.at[source, part], s1.at[i], r1.at[i], d, to)))
    for i in range(1, owners):
        to = (c + i) % owners
        move(e, eg, c, (c + owners - i) % owners, se.at[i], re.at[i], (d, to))
    for copy in local:
        copy.start()
    finish(ended, local)


def spread(h, e, u, lab, doms, owners, fine):
    plane = doms * fine
    dma = pltpu.SemaphoreType.DMA
    anywhere = pl.BlockSpec(memory_space=pl.ANY)
    return pl.pallas_call(
        functools.partial(spread_kernel, doms, owners, fine),
        out_shape=(
            jax.ShapeDtypeStruct((owners,) + h.shape, h.dtype),
            jax.ShapeDtypeStruct((owners,) + e.shape, e.dtype),
            jax.ShapeDtypeStruct(u.shape, u.dtype),
            jax.ShapeDtypeStruct((plane,) + lab.shape, lab.dtype),
        ),
        in_specs=[pl.BlockSpec(memory_space=pltpu.VMEM)] * 4,
        out_specs=(anywhere,) * 4,
        scratch_shapes=[dma((owners,))] * 4 + [dma((plane,))] * 4 + [dma((4,))],
        compiler_params=pltpu.CompilerParams(collective_id=0, has_side_effects=True),
    )(h, e, u, lab)


def owner_kernel(
    owners, fine, hg_in, sums, den, hg, sums_out, den_out,
    sx, rx, sy, ry, sm, rm, s1, r1, s2, r2, own,
):
    d, c, side, row, across, mate = place(hg)
    quarter = hg.shape[1] // 4
    half = 2 * quarter
    mine = pl.ds((side * 2 + row) * quarter, quarter)
    theirs = pl.ds((side * 2 + 1 - row) * quarter, quarter)
    here = pl.ds(side * half, half)
    there = pl.ds((1 - side) * half, half)
    lines = owners // fine
    barrier = pltpu.get_barrier_semaphore()
    for i in range(1, owners):
        signal_to(barrier, d, (c + i) % owners)
    signal_to(barrier, across, c)
    signal_to(barrier, mate, c)
    pl.semaphore_wait(barrier, owners + 1)
    local = [
        pltpu.make_async_copy(sums.at[c], sums_out.at[c], own.at[0]),
        pltpu.make_async_copy(den.at[c], den_out.at[c], own.at[1]),
    ]
    ended = []

    def shard(col, line):
        return (c - c % fine + line * fine + (c % fine + col) % fine) % owners

    def send(source, taken, part, other, sems, to):
        piece = hg.at[source, part]
        sent = remote(piece, piece, sems[0], sems[1], *to)
        sent.start()
        arrival = remote(piece, hg.at[taken, other], sems[0], sems[1], *to)
        ended.append((sent, arrival))
        return arrival

    def to_across(source, k):
        return send(source, source, mine, theirs, (sy.at[k], ry.at[k]), (across, c))

    def to_mate(source, k):
        send(source, source, here, there, (sm.at[k], rm.at[k]), (mate, c))

    from_side = []
    for col in range(1, fine):
        to = (d, c - c % fine + (c % fine + col) % fine)
        back = (fine - col) % fine
        for line in range(lines):
            k = col * lines + line
            from_side.append(
                (
                    shard(back, line),
                    k,
                    send(
                        shard(0, line),
                        shard(back, line),
                        mine,
                        mine,
                        (sx.at[k], rx.at[k]),
                        to,
                    ),
                )
            )
    waiting = []
    for line in range(1, lines):
        waiting.append((shard(0, line), line, to_across(shard(0, line), line)))
    for i in range(1, owners):
        to = (c + i) % owners
        source = (c + owners - i) % owners
        for src, dst, out, into in ((sums, sums_out, s1, r1), (den, den_out, s2, r2)):
            sent = remote(src.at[to], dst.at[c], out.at[i], into.at[i], d, to)
            sent.start()
            ended.append((sent, remote(src.at[to], dst.at[source], out.at[i], into.at[i], d, to)))
    for copy in local:
        copy.start()
    seen = set()
    for source, k, arrival in from_side:
        arrival.wait_recv()
        seen.add(id(arrival))
        waiting.append((source, k, to_across(source, k)))
        ready = waiting.pop(0)
        ready[2].wait_recv()
        seen.add(id(ready[2]))
        to_mate(ready[0], ready[1])
    for source, k, arrival in waiting:
        arrival.wait_recv()
        seen.add(id(arrival))
        to_mate(source, k)
    for sent, arrival in ended:
        sent.wait_send()
        if id(arrival) not in seen:
            arrival.wait_recv()
    for copy in local:
        copy.wait()


def to_owners(hg, sums, den, owners, fine):
    dma = pltpu.SemaphoreType.DMA
    anywhere = pl.BlockSpec(memory_space=pl.ANY)
    return pl.pallas_call(
        functools.partial(owner_kernel, owners, fine),
        out_shape=(
            jax.ShapeDtypeStruct(hg.shape, hg.dtype),
            jax.ShapeDtypeStruct(sums.shape, sums.dtype),
            jax.ShapeDtypeStruct(den.shape, den.dtype),
        ),
        in_specs=[anywhere] + [pl.BlockSpec(memory_space=pltpu.VMEM)] * 2,
        out_specs=(anywhere,) * 3,
        input_output_aliases={0: 0},
        scratch_shapes=[dma((owners,))] * 10 + [dma((2,))],
        compiler_params=pltpu.CompilerParams(collective_id=1, has_side_effects=True),
    )(hg, sums, den)


def largest_turn(take):
    columns = [[None] * 9 for _ in range(4)]
    for m2 in range(9):
        real, imag = [], []
        for m1 in range(4):
            x, y = take((9 * m1 + 4 * m2) % 36)
            real.append(x)
            imag.append(y)
        ar, ai = real[0] + real[2], imag[0] + imag[2]
        br, bi = real[0] - real[2], imag[0] - imag[2]
        cr, ci = real[1] + real[3], imag[1] + imag[3]
        dr, di = real[1] - real[3], imag[1] - imag[3]
        columns[0][m2] = (ar + cr, ai + ci)
        columns[1][m2] = (br + di, bi - dr)
        columns[2][m2] = (ar - cr, ai - ci)
        columns[3][m2] = (br - di, bi + dr)
    best = None
    for x in columns:
        even = [x[b][0] + x[9 - b][0] for b in range(1, 5)]
        odd = [x[b][1] - x[9 - b][1] for b in range(1, 5)]
        tops = [x[0][0] + even[0] + even[1] + even[2] + even[3]]
        for s in range(1, 5):
            total = x[0][0]
            turn = None
            for b in range(1, 5):
                step = 2.0 * math.pi * (b * s % 9) / 9
                total = total + even[b - 1] * math.cos(step)
                term = odd[b - 1] * math.sin(step)
                turn = term if turn is None else turn + term
            tops.append(total + jnp.abs(turn))
        for top in tops:
            best = top if best is None else jnp.maximum(best, top)
    return best


def score_kernel(per_owner, lhs, hg, scale, out, folded, best):
    step = pl.program_id(0)
    owners, _, _, depth = hg.shape
    group, rows, _ = lhs.shape
    count = rows // 2
    width = folded.shape[2]
    main = per_owner // 8 * 8
    rest = per_owner - main
    tails = [hg[o, 0, group * main :, :].astype(jnp.float32) for o in range(owners)]
    for g in range(group):
        parts = [
            hg[o, 0, g * main : (g + 1) * main, :].astype(jnp.float32) for o in range(owners)
        ]
        parts += [tails[o][g * rest + k : g * rest + k + 1] for o in range(owners) for k in range(rest)]
        if width > owners * per_owner:
            parts.append(jnp.zeros((width - owners * per_owner, depth), jnp.float32))
        block = jnp.concatenate(parts, axis=0).astype(jnp.bfloat16)
        folded[step * group + g] = lax.dot_general(
            lhs[g], block, (((1,), (1,)), ((), ())), preferred_element_type=jnp.float32
        )

    @pl.when(step == pl.num_programs(0) - 1)
    def _():
        def tile(t, carry):
            at = pl.ds(pl.multiple_of(t * 8, 8), 8)
            after = pl.ds(pl.multiple_of(count + t * 8, 8), 8)
            for lane in range(width // 128):
                cols = pl.ds(lane * 128, 128)

                def take(m):
                    return folded[m, at, cols], folded[m, after, cols]

                best[at, cols] = largest_turn(take)
            return carry

        lax.fori_loop(0, count // 8, tile, 0)
        power = scale[...]
        scores = jnp.where(power < 0.0, -1e30, best[...] * power)
        out[...] = jnp.broadcast_to(jnp.max(scores, axis=1, keepdims=True), out.shape)


def best_scores(lhs, hg, scale, per_owner):
    turns, rows, depth = lhs.shape
    owners, pieces, packed, _ = hg.shape
    width = scale.shape[1]
    group = turns // pieces
    return pl.pallas_call(
        functools.partial(score_kernel, per_owner),
        grid=(pieces,),
        out_shape=jax.ShapeDtypeStruct((rows // 2, 128), jnp.float32),
        in_specs=[
            pl.BlockSpec((group, rows, depth), lambda i: (i, 0, 0)),
            pl.BlockSpec((owners, 1, packed, depth), lambda i: (0, i, 0, 0)),
            pl.BlockSpec((rows // 2, width), lambda i: (0, 0)),
        ],
        out_specs=pl.BlockSpec((rows // 2, 128), lambda i: (0, 0)),
        scratch_shapes=[
            pltpu.VMEM((turns, rows, width), jnp.float32),
            pltpu.VMEM((rows // 2, width), jnp.float32),
        ],
        compiler_params=pltpu.CompilerParams(vmem_limit_bytes=48 * 1024 * 1024),
    )(lhs, hg, scale)[:, 0]


def on_device(particles, references, class_block, class_local, rotation, shifts, defocus):
    particle_count, cycle_count, row_width = particles.shape
    angles = row_width // 2
    copies = angles // ROT
    dom_count = lax.axis_size("dom")
    owners = lax.axis_size("cls")
    per_owner = references.shape[0]
    padded = -(-per_owner // 16) * 16
    fine = 2 if owners % 2 == 0 else 1
    plane = dom_count * fine
    thin = cycle_count // plane
    contrast, shifted, unrotated = prepare(particles, rotation, shifts, defocus)
    table = angle_table(angles).T
    lhs, _ = rotation_major(shifted, contrast, table, copies, 0)
    major, energy = rotation_major(
        jnp.pad(references, ((0, padded - per_owner), (0, 0), (0, 0))),
        jnp.ones((padded, cycle_count), jnp.float32),
        table,
        copies,
        per_owner,
    )
    energy = jnp.pad(energy, ((0, 0), (0, -cycle_count % 128)))
    outbox = (
        unrotated.reshape(particle_count, plane, thin * row_width).transpose(1, 0, 2)
    )
    class_ids = class_block[:, 0] * per_owner + class_local
    labels = jnp.pad(jnp.stack([class_ids, defocus]), ((0, 6), (0, -particle_count % 128)))
    all_major, all_energy, inbox, inbox_labels = spread(
        major, energy, outbox, labels, dom_count, owners, fine
    )
    ids = inbox_labels[:, 0, :particle_count].reshape(-1)
    bins = inbox_labels[:, 1, :particle_count].reshape(-1)
    member = jnp.arange(owners * per_owner, dtype=jnp.int32)[:, None] == ids[None, :]
    sums = jnp.dot(
        member.astype(jnp.bfloat16),
        inbox.reshape(plane * particle_count, thin * row_width),
        preferred_element_type=jnp.float32,
    ).astype(jnp.bfloat16)
    slab = lax.axis_index("dom") * fine + lax.axis_index("cls") % fine
    table = ctf_table(NBINS, cycle_count)
    table = lax.dynamic_slice_in_dim(table * table, slab * thin, thin, 1)
    hits = (bins[:, None] == jnp.arange(NBINS, dtype=jnp.int32)[None, :]).astype(jnp.float32)
    squares = jnp.dot(hits, table, precision=lax.Precision.HIGHEST)
    den = jnp.dot(member.astype(jnp.float32), squares, precision=lax.Precision.HIGHEST)
    den = den.reshape(owners, per_owner, thin).transpose(0, 2, 1)
    den = jnp.pad(den, ((0, 0), (0, -thin % 8), (0, -per_owner % 128)))
    all_major, all_sums, all_den = to_owners(
        all_major, sums.reshape(owners, per_owner, thin * row_width), den, owners, fine
    )
    numerator = lax.optimization_barrier(
        jnp.sum(
            all_sums.astype(jnp.float32).reshape(
                owners // fine, fine, per_owner, thin * row_width
            ),
            axis=0,
        )
    ).reshape(fine, per_owner, thin, row_width)
    denominator = jnp.sum(
        all_den[:, :thin, :per_owner].reshape(owners // fine, fine, thin, per_owner), axis=0
    ).transpose(0, 2, 1)
    class_average = numerator / (denominator[:, :, :, None] + 1.0)
    class_average = class_average.transpose(1, 0, 2, 3).reshape(
        per_owner, fine * thin, row_width
    )
    main = per_owner // 8 * 8
    energies = jnp.concatenate(
        [
            all_energy[:, :main, :cycle_count].reshape(-1, cycle_count),
            all_energy[:, main:per_owner, :cycle_count].reshape(-1, cycle_count),
        ],
        axis=0,
    )
    power = jnp.dot(contrast * contrast, energies.T, precision=lax.Precision.HIGHEST) / angles
    scale = jnp.pad(
        1.0 / (angles * jnp.sqrt(power + EPSILON)),
        ((0, 0), (0, -owners * per_owner % 128)),
        constant_values=-1.0,
    )
    return (best_scores(lhs, all_major, scale, per_owner), class_average)


def solution(mesh):
    placed = (
        P(("dom", "cls"), None, None),
        P("cls", None, None),
        P(("dom", "cls"), None),
        P(("dom", "cls")),
        P(("dom", "cls")),
        P(("dom", "cls"), None),
        P(("dom", "cls")),
    )
    return jax.shard_map(
        on_device,
        mesh=mesh,
        in_specs=placed,
        out_specs=(P(("dom", "cls")), P("cls", "dom", None)),
        check_vma=False,
    )
```

```python
import functools
import math

import jax
import jax.numpy as jnp
from jax import lax
from jax.experimental import pallas as pl
from jax.experimental.pallas import tpu as pltpu
from jax.sharding import PartitionSpec as P

ROT = 36
BOX = 128
NBINS = 16


EPSILON = 1e-06


def angle_table(angles):
    sample_index = jnp.arange(angles, dtype=jnp.int32)
    turn_count = sample_index[:, None] * sample_index[None, :] % angles
    angle_value = turn_count.astype(jnp.float32) * (2.0 * math.pi / angles)
    cosine = jnp.cos(angle_value)
    sine_part = jnp.sin(angle_value)
    upper_half = jnp.concatenate([cosine, -sine_part], axis=1)
    lower_half = jnp.concatenate([sine_part, cosine], axis=1)
    return jnp.concatenate([upper_half, lower_half], axis=0).astype(jnp.bfloat16)


def ctf_table(bins, cycle_count):
    radius = (jnp.arange(cycle_count, dtype=jnp.int32) + 1).astype(jnp.float32) / cycle_count
    defocus_level = jnp.arange(bins, dtype=jnp.int32).astype(jnp.float32) / bins
    phase = math.pi * (3.0 + 9.0 * defocus_level[:, None]) * (radius[None, :] * radius[None, :])
    return 0.995 * jnp.sin(phase) + 0.1 * jnp.cos(phase)


def ctf_rows(defocus, bins, cycle_count):
    defocus_hits = (defocus[:, None] == jnp.arange(bins, dtype=jnp.int32)[None, :]).astype(
        jnp.float32
    )
    return jnp.dot(defocus_hits, ctf_table(bins, cycle_count), precision=lax.Precision.HIGHEST)


def phase_turns(shifts, cycle_count, angles):
    inner = 8
    outer = cycle_count // inner
    angle_value = jnp.arange(angles, dtype=jnp.int32).astype(jnp.float32) * (2.0 * math.pi / angles)
    along = (
        shifts[:, 0].astype(jnp.float32)[:, None] * jnp.cos(angle_value)[None, :]
        + shifts[:, 1].astype(jnp.float32)[:, None] * jnp.sin(angle_value)[None, :]
    ) * (2.0 * math.pi / BOX)
    fine = jnp.arange(inner, dtype=jnp.int32).astype(jnp.float32)[None, :, None] * along[:, None, :]
    coarse = (jnp.arange(outer, dtype=jnp.int32) * inner).astype(jnp.float32)[
        None, :, None
    ] * along[:, None, :]
    cf, sf = jnp.cos(fine)[:, None], jnp.sin(fine)[:, None]
    cc, sc = jnp.cos(coarse)[:, :, None], jnp.sin(coarse)[:, :, None]
    shape = (shifts.shape[0], cycle_count, angles)
    return (cf * cc - sf * sc).reshape(shape), (sf * cc + cf * sc).reshape(shape)


def prepare(particles, rotation, shifts, defocus):
    particle_count, cycle_count, row_width = particles.shape
    angles = row_width // 2
    cos_phase, sin_phase = phase_turns(shifts, cycle_count, angles)
    real_part = particles[:, :, :angles].astype(jnp.float32)
    imag_part = particles[:, :, angles:].astype(jnp.float32)
    shifted = jnp.concatenate(
        [
            real_part * cos_phase - imag_part * sin_phase,
            real_part * sin_phase + imag_part * cos_phase,
        ],
        axis=2,
    ).astype(jnp.bfloat16)
    spectrum = jnp.dot(
        shifted.reshape(particle_count * cycle_count, row_width),
        angle_table(angles),
        preferred_element_type=jnp.float32,
    ).reshape(particle_count, cycle_count, row_width)
    contrast = ctf_rows(defocus, NBINS, cycle_count)
    rotate_step = angles // ROT
    harmonic = jnp.arange(angles, dtype=jnp.int32)
    turn_count = harmonic[None, :] * (rotate_step * rotation[:, None]) % angles
    angle_value = turn_count.astype(jnp.float32) * (2.0 * math.pi / angles)
    cos_rot = jnp.cos(angle_value)[:, None, :]
    sin_rot = jnp.sin(angle_value)[:, None, :]
    spec_real = spectrum[:, :, :angles]
    spec_imag = spectrum[:, :, angles:]
    turned = jnp.concatenate(
        [spec_real * cos_rot - spec_imag * sin_rot, spec_real * sin_rot + spec_imag * cos_rot],
        axis=2,
    )
    unrotated = (contrast[:, :, None] * turned).astype(jnp.bfloat16)
    return (contrast, shifted, unrotated)


def major_kernel(copies, packed, rows, gain, table, out, energy, wide, dense=None):
    pairs, lanes = gain.shape
    width = table.shape[0]
    turns = width // 2 // copies
    cycles = lanes // 2

    def transform(i, carry):
        both_rows = jnp.concatenate([rows[i], rows[pairs + i]], axis=0)
        spectrum = lax.dot_general(
            table[...],
            both_rows,
            (((1,), (1,)), ((), ())),
            preferred_element_type=jnp.float32,
        )
        spectrum = (spectrum * gain[pl.ds(i, 1), :]).astype(jnp.bfloat16).astype(jnp.float32)
        energy[pl.ds(i, 1), :] = jnp.sum(spectrum * spectrum, axis=0, keepdims=True)
        wide[pl.ds(i, width, stride=pairs), :] = spectrum
        return carry

    lax.fori_loop(0, pairs, transform, 0, unroll=4)
    low = lax.broadcasted_iota(jnp.int32, (pairs, lanes), 1) < cycles

    def gather(m, carry):
        def part(index):
            at = (index * turns + m) * pairs
            return wide[pl.ds(pl.multiple_of(at, 8), pairs), :]

        tops, ends = [], []
        for index in range(0, 2 * copies, 2):
            x, y = part(index), part(index + 1)
            tops.append(jnp.where(low, x, pltpu.roll(y, cycles, 1)))
            ends.append(jnp.where(low, pltpu.roll(x, cycles, 1), y))
        half = len(tops) // 2
        full = jnp.concatenate(
            [jnp.concatenate(tops, axis=1), jnp.concatenate(ends, axis=1)], axis=0
        )
        if packed:
            main = packed // 8 * 8
            group = turns // 4
            start = m // group * out.shape[1]
            turn = m % group
            at = pl.multiple_of(start + turn * main, 8)
            dense[pl.ds(at, main), :] = full[:main]
            for k in range(main, packed):
                at = start + group * main + turn * (packed - main) + k - main
                dense[pl.ds(at, 1), :] = full[k : k + 1]
        else:
            out[m, pl.ds(0, 2 * pairs), :] = full.astype(out.dtype)
            tops = [-x for x in tops[half:]] + tops[:half]
            ends = [-x for x in ends[half:]] + ends[:half]
            full = jnp.concatenate(
                [jnp.concatenate(tops, axis=1), jnp.concatenate(ends, axis=1)], axis=0
            )
            out[m, pl.ds(2 * pairs, 2 * pairs), :] = full.astype(out.dtype)
        return carry

    if packed:
        dense[...] = jnp.zeros_like(dense)
    lax.fori_loop(0, turns, gather, 0, unroll=4)
    if packed:
        out[...] = dense[...].reshape(out.shape).astype(out.dtype)


def rotation_major(rows, gain, table, copies, packed):
    count, cycles, width = rows.shape
    pairs = count // 2
    turns = width // 2 // copies
    paired = jnp.concatenate([gain[:pairs], gain[pairs:]], axis=1)
    depth = 2 * copies * cycles
    scratch = [pltpu.VMEM((width * pairs, 2 * cycles), jnp.float32)]
    shape = (turns, 2 * count, depth)
    if packed:
        shape = (4, -(-(turns // 4 * packed) // 8) * 8, depth)
        scratch.append(pltpu.VMEM((shape[0] * shape[1], depth), jnp.float32))
    out, energy = pl.pallas_call(
        functools.partial(major_kernel, copies, packed),
        out_shape=(
            jax.ShapeDtypeStruct(shape, rows.dtype),
            jax.ShapeDtypeStruct((pairs, 2 * cycles), jnp.float32),
        ),
        in_specs=[pl.BlockSpec(memory_space=pltpu.VMEM)] * 3,
        out_specs=(pl.BlockSpec(memory_space=pltpu.VMEM),) * 2,
        scratch_shapes=scratch,
        compiler_params=pltpu.CompilerParams(vmem_limit_bytes=32 * 1024 * 1024),
    )(rows, paired, table)
    return out, jnp.concatenate([energy[:, :cycles], energy[:, cycles:]], axis=0)


def remote(src, dst, send, recv, d, c):
    return pltpu.make_async_remote_copy(
        src_ref=src,
        dst_ref=dst,
        send_sem=send,
        recv_sem=recv,
        device_id=(d, c),
        device_id_type=pl.DeviceIdType.MESH,
    )


def place(h):
    d = lax.axis_index("dom")
    c = lax.axis_index("cls")
    inner = d % 4
    base = d - inner
    side = inner % 2
    row = inner // 2
    across = base + (1 - row) * 2 + side
    mate = base + row * 2 + (1 - side)
    return d, c, side, row, across, mate


def signal_to(barrier, d, c):
    pl.semaphore_signal(barrier, inc=1, device_id=(d, c), device_id_type=pl.DeviceIdType.MESH)


def finish(ended, local):
    for sent, arrival in ended:
        sent.wait_send()
        arrival.wait_recv()
    for copy in local:
        copy.wait()


def spread_kernel(
    doms, owners, fine, h, e, u, lab, hg, eg, ug, lg, s1, r1, se, re, su, ru, sl, rl, own
):
    d, c, side, row, across, mate = place(h)
    quarter = h.shape[0] // 4
    piece = (side * 2 + row) * quarter
    lines = owners // fine
    plane = doms * fine
    slab = d * fine + c % fine
    first = c - c % fine
    barrier = pltpu.get_barrier_semaphore()
    for i in range(1, owners):
        signal_to(barrier, d, (c + i) % owners)
    for i in range(1, plane):
        other = (slab + i) % plane
        signal_to(barrier, other // fine, first + other % fine)
    pl.semaphore_wait(barrier, owners - 1 + plane - 1)
    local = [
        pltpu.make_async_copy(h, hg.at[c], own.at[0]),
        pltpu.make_async_copy(e, eg.at[c], own.at[1]),
        pltpu.make_async_copy(u.at[slab], ug.at[slab], own.at[2]),
        pltpu.make_async_copy(lab, lg.at[slab], own.at[3]),
    ]
    ended = []

    def move(src, dst, at, source, send, recv, to):
        sent = remote(src, dst.at[at], send, recv, *to)
        sent.start()
        ended.append((sent, remote(src, dst.at[source], send, recv, *to)))

    part = pl.ds(piece, quarter)
    for i in range(1, lines):
        to = (c + i * fine) % owners
        source = (c + owners - i * fine) % owners
        sent = remote(h.at[part], hg.at[c, part], s1.at[i], r1.at[i], d, to)
        sent.start()
        ended.append((sent, remote(h.at[part], hg.at[source, part], s1.at[i], r1.at[i], d, to)))
    for i in range(1, plane):
        other = (slab + i) % plane
        source = (slab + plane - i) % plane
        to = (other // fine, first + other % fine)
        move(lab, lg, slab, source, sl.at[i], rl.at[i], to)
        move(u.at[other], ug, slab, source, su.at[i], ru.at[i], to)
    for i in range(1, owners):
        to = (c + i) % owners
        move(e, eg, c, (c + owners - i) % owners, se.at[i], re.at[i], (d, to))
    for copy in local:
        copy.start()
    finish(ended, local)


def spread(h, e, u, lab, doms, owners, fine):
    plane = doms * fine
    dma = pltpu.SemaphoreType.DMA
    anywhere = pl.BlockSpec(memory_space=pl.ANY)
    return pl.pallas_call(
        functools.partial(spread_kernel, doms, owners, fine),
        out_shape=(
            jax.ShapeDtypeStruct((owners,) + h.shape, h.dtype),
            jax.ShapeDtypeStruct((owners,) + e.shape, e.dtype),
            jax.ShapeDtypeStruct(u.shape, u.dtype),
            jax.ShapeDtypeStruct((plane,) + lab.shape, lab.dtype),
        ),
        in_specs=[pl.BlockSpec(memory_space=pltpu.VMEM)] * 4,
        out_specs=(anywhere,) * 4,
        scratch_shapes=[dma((owners,))] * 4 + [dma((plane,))] * 4 + [dma((4,))],
        compiler_params=pltpu.CompilerParams(collective_id=0, has_side_effects=True),
    )(h, e, u, lab)


def owner_kernel(
    owners, fine, hg_in, sums, den, hg, sums_out, den_out,
    sx, rx, sy, ry, sm, rm, s1, r1, s2, r2, own,
):
    d, c, side, row, across, mate = place(hg)
    quarter = hg.shape[1] // 4
    half = 2 * quarter
    mine = pl.ds((side * 2 + row) * quarter, quarter)
    theirs = pl.ds((side * 2 + 1 - row) * quarter, quarter)
    here = pl.ds(side * half, half)
    there = pl.ds((1 - side) * half, half)
    lines = owners // fine
    barrier = pltpu.get_barrier_semaphore()
    for i in range(1, owners):
        signal_to(barrier, d, (c + i) % owners)
    signal_to(barrier, across, c)
    signal_to(barrier, mate, c)
    pl.semaphore_wait(barrier, owners + 1)
    local = [
        pltpu.make_async_copy(sums.at[c], sums_out.at[c], own.at[0]),
        pltpu.make_async_copy(den.at[c], den_out.at[c], own.at[1]),
    ]
    ended = []

    def shard(col, line):
        return (c - c % fine + line * fine + (c % fine + col) % fine) % owners

    def send(source, taken, part, other, sems, to):
        piece = hg.at[source, part]
        sent = remote(piece, piece, sems[0], sems[1], *to)
        sent.start()
        arrival = remote(piece, hg.at[taken, other], sems[0], sems[1], *to)
        ended.append((sent, arrival))
        return arrival

    def to_across(source, k):
        return send(source, source, mine, theirs, (sy.at[k], ry.at[k]), (across, c))

    def to_mate(source, k):
        send(source, source, here, there, (sm.at[k], rm.at[k]), (mate, c))

    waiting = []
    for line in range(1, lines):
        waiting.append((shard(0, line), line, to_across(shard(0, line), line)))
    from_side = []
    for col in range(1, fine):
        to = (d, c - c % fine + (c % fine + col) % fine)
        back = (fine - col) % fine
        for line in range(lines):
            k = col * lines + line
            from_side.append(
                (
                    shard(back, line),
                    k,
                    send(
                        shard(0, line),
                        shard(back, line),
                        mine,
                        mine,
                        (sx.at[k], rx.at[k]),
                        to,
                    ),
                )
            )
    for i in range(1, owners):
        to = (c + i) % owners
        source = (c + owners - i) % owners
        for src, dst, out, into in ((sums, sums_out, s1, r1), (den, den_out, s2, r2)):
            sent = remote(src.at[to], dst.at[c], out.at[i], into.at[i], d, to)
            sent.start()
            ended.append((sent, remote(src.at[to], dst.at[source], out.at[i], into.at[i], d, to)))
    for copy in local:
        copy.start()
    seen = set()
    for source, k, arrival in from_side:
        arrival.wait_recv()
        seen.add(id(arrival))
        waiting.append((source, k, to_across(source, k)))
        ready = waiting.pop(0)
        ready[2].wait_recv()
        seen.add(id(ready[2]))
        to_mate(ready[0], ready[1])
    for source, k, arrival in waiting:
        arrival.wait_recv()
        seen.add(id(arrival))
        to_mate(source, k)
    for sent, arrival in ended:
        sent.wait_send()
        if id(arrival) not in seen:
            arrival.wait_recv()
    for copy in local:
        copy.wait()


def to_owners(hg, sums, den, owners, fine):
    dma = pltpu.SemaphoreType.DMA
    anywhere = pl.BlockSpec(memory_space=pl.ANY)
    return pl.pallas_call(
        functools.partial(owner_kernel, owners, fine),
        out_shape=(
            jax.ShapeDtypeStruct(hg.shape, hg.dtype),
            jax.ShapeDtypeStruct(sums.shape, sums.dtype),
            jax.ShapeDtypeStruct(den.shape, den.dtype),
        ),
        in_specs=[anywhere] + [pl.BlockSpec(memory_space=pltpu.VMEM)] * 2,
        out_specs=(anywhere,) * 3,
        input_output_aliases={0: 0},
        scratch_shapes=[dma((owners,))] * 10 + [dma((2,))],
        compiler_params=pltpu.CompilerParams(collective_id=1, has_side_effects=True),
    )(hg, sums, den)


def largest_turn(take):
    columns = [[None] * 9 for _ in range(4)]
    for m2 in range(9):
        real, imag = [], []
        for m1 in range(4):
            x, y = take((9 * m1 + 4 * m2) % 36)
            real.append(x)
            imag.append(y)
        ar, ai = real[0] + real[2], imag[0] + imag[2]
        br, bi = real[0] - real[2], imag[0] - imag[2]
        cr, ci = real[1] + real[3], imag[1] + imag[3]
        dr, di = real[1] - real[3], imag[1] - imag[3]
        columns[0][m2] = (ar + cr, ai + ci)
        columns[1][m2] = (br + di, bi - dr)
        columns[2][m2] = (ar - cr, ai - ci)
        columns[3][m2] = (br - di, bi + dr)
    best = None
    for x in columns:
        even = [x[b][0] + x[9 - b][0] for b in range(1, 5)]
        odd = [x[b][1] - x[9 - b][1] for b in range(1, 5)]
        tops = [x[0][0] + even[0] + even[1] + even[2] + even[3]]
        for s in range(1, 5):
            total = x[0][0]
            turn = None
            for b in range(1, 5):
                step = 2.0 * math.pi * (b * s % 9) / 9
                total = total + even[b - 1] * math.cos(step)
                term = odd[b - 1] * math.sin(step)
                turn = term if turn is None else turn + term
            tops.append(total + jnp.abs(turn))
        for top in tops:
            best = top if best is None else jnp.maximum(best, top)
    return best


def score_kernel(per_owner, lhs, hg, scale, out, folded, best):
    step = pl.program_id(0)
    owners, _, _, depth = hg.shape
    group, rows, _ = lhs.shape
    count = rows // 2
    width = folded.shape[2]
    main = per_owner // 8 * 8
    rest = per_owner - main
    tails = [hg[o, 0, group * main :, :].astype(jnp.float32) for o in range(owners)]
    for g in range(group):
        parts = [
            hg[o, 0, g * main : (g + 1) * main, :].astype(jnp.float32) for o in range(owners)
        ]
        parts += [tails[o][g * rest + k : g * rest + k + 1] for o in range(owners) for k in range(rest)]
        if width > owners * per_owner:
            parts.append(jnp.zeros((width - owners * per_owner, depth), jnp.float32))
        block = jnp.concatenate(parts, axis=0).astype(jnp.bfloat16)
        folded[step * group + g] = lax.dot_general(
            lhs[g], block, (((1,), (1,)), ((), ())), preferred_element_type=jnp.float32
        )

    @pl.when(step == pl.num_programs(0) - 1)
    def _():
        def tile(t, carry):
            at = pl.ds(pl.multiple_of(t * 8, 8), 8)
            after = pl.ds(pl.multiple_of(count + t * 8, 8), 8)
            for lane in range(width // 128):
                cols = pl.ds(lane * 128, 128)

                def take(m):
                    return folded[m, at, cols], folded[m, after, cols]

                best[at, cols] = largest_turn(take)
            return carry

        lax.fori_loop(0, count // 8, tile, 0)
        power = scale[...]
        scores = jnp.where(power < 0.0, -1e30, best[...] * power)
        out[...] = jnp.broadcast_to(jnp.max(scores, axis=1, keepdims=True), out.shape)


def best_scores(lhs, hg, scale, per_owner):
    turns, rows, depth = lhs.shape
    owners, pieces, packed, _ = hg.shape
    width = scale.shape[1]
    group = turns // pieces
    return pl.pallas_call(
        functools.partial(score_kernel, per_owner),
        grid=(pieces,),
        out_shape=jax.ShapeDtypeStruct((rows // 2, 128), jnp.float32),
        in_specs=[
            pl.BlockSpec((group, rows, depth), lambda i: (i, 0, 0)),
            pl.BlockSpec((owners, 1, packed, depth), lambda i: (0, i, 0, 0)),
            pl.BlockSpec((rows // 2, width), lambda i: (0, 0)),
        ],
        out_specs=pl.BlockSpec((rows // 2, 128), lambda i: (0, 0)),
        scratch_shapes=[
            pltpu.VMEM((turns, rows, width), jnp.float32),
            pltpu.VMEM((rows // 2, width), jnp.float32),
        ],
        compiler_params=pltpu.CompilerParams(vmem_limit_bytes=48 * 1024 * 1024),
    )(lhs, hg, scale)[:, 0]


def on_device(particles, references, class_block, class_local, rotation, shifts, defocus):
    particle_count, cycle_count, row_width = particles.shape
    angles = row_width // 2
    copies = angles // ROT
    dom_count = lax.axis_size("dom")
    owners = lax.axis_size("cls")
    per_owner = references.shape[0]
    padded = -(-per_owner // 16) * 16
    fine = 2 if owners % 2 == 0 else 1
    plane = dom_count * fine
    thin = cycle_count // plane
    contrast, shifted, unrotated = prepare(particles, rotation, shifts, defocus)
    table = angle_table(angles).T
    lhs, _ = rotation_major(shifted, contrast, table, copies, 0)
    major, energy = rotation_major(
        jnp.pad(references, ((0, padded - per_owner), (0, 0), (0, 0))),
        jnp.ones((padded, cycle_count), jnp.float32),
        table,
        copies,
        per_owner,
    )
    energy = jnp.pad(energy, ((0, 0), (0, -cycle_count % 128)))
    outbox = (
        unrotated.reshape(particle_count, plane, thin * row_width).transpose(1, 0, 2)
    )
    class_ids = class_block[:, 0] * per_owner + class_local
    labels = jnp.pad(jnp.stack([class_ids, defocus]), ((0, 6), (0, -particle_count % 128)))
    all_major, all_energy, inbox, inbox_labels = spread(
        major, energy, outbox, labels, dom_count, owners, fine
    )
    ids = inbox_labels[:, 0, :particle_count].reshape(-1)
    bins = inbox_labels[:, 1, :particle_count].reshape(-1)
    member = jnp.arange(owners * per_owner, dtype=jnp.int32)[:, None] == ids[None, :]
    sums = jnp.dot(
        member.astype(jnp.bfloat16),
        inbox.reshape(plane * particle_count, thin * row_width),
        preferred_element_type=jnp.float32,
    ).astype(jnp.bfloat16)
    slab = lax.axis_index("dom") * fine + lax.axis_index("cls") % fine
    table = ctf_table(NBINS, cycle_count)
    table = lax.dynamic_slice_in_dim(table * table, slab * thin, thin, 1)
    hits = (bins[:, None] == jnp.arange(NBINS, dtype=jnp.int32)[None, :]).astype(jnp.float32)
    squares = jnp.dot(hits, table, precision=lax.Precision.HIGHEST)
    den = jnp.dot(member.astype(jnp.float32), squares, precision=lax.Precision.HIGHEST)
    den = den.reshape(owners, per_owner, thin).transpose(0, 2, 1)
    den = jnp.pad(den, ((0, 0), (0, -thin % 8), (0, -per_owner % 128)))
    all_major, all_sums, all_den = to_owners(
        all_major, sums.reshape(owners, per_owner, thin * row_width), den, owners, fine
    )
    numerator = lax.optimization_barrier(
        jnp.sum(
            all_sums.astype(jnp.float32).reshape(
                owners // fine, fine, per_owner, thin * row_width
            ),
            axis=0,
        )
    ).reshape(fine, per_owner, thin, row_width)
    denominator = jnp.sum(
        all_den[:, :thin, :per_owner].reshape(owners // fine, fine, thin, per_owner), axis=0
    ).transpose(0, 2, 1)
    class_average = numerator / (denominator[:, :, :, None] + 1.0)
    class_average = class_average.transpose(1, 0, 2, 3).reshape(
        per_owner, fine * thin, row_width
    )
    main = per_owner // 8 * 8
    energies = jnp.concatenate(
        [
            all_energy[:, :main, :cycle_count].reshape(-1, cycle_count),
            all_energy[:, main:per_owner, :cycle_count].reshape(-1, cycle_count),
        ],
        axis=0,
    )
    power = jnp.dot(contrast * contrast, energies.T, precision=lax.Precision.HIGHEST) / angles
    scale = jnp.pad(
        1.0 / (angles * jnp.sqrt(power + EPSILON)),
        ((0, 0), (0, -owners * per_owner % 128)),
        constant_values=-1.0,
    )
    return (best_scores(lhs, all_major, scale, per_owner), class_average)


def solution(mesh):
    placed = (
        P(("dom", "cls"), None, None),
        P("cls", None, None),
        P(("dom", "cls"), None),
        P(("dom", "cls")),
        P(("dom", "cls")),
        P(("dom", "cls"), None),
        P(("dom", "cls")),
    )
    return jax.shard_map(
        on_device,
        mesh=mesh,
        in_specs=placed,
        out_specs=(P(("dom", "cls")), P("cls", "dom", None)),
        check_vma=False,
    )
```
